128 devices in a mesh: comp: 4 (over x), blk: 32 (over y, z, core).
Axes of the slice: x: 4, y: 4, z: 4, core: 2. Of those that a mesh axis runs over, the one named last changes fastest.
Arguments:
- psi_start: float32 [4, 6, 256, 128, 128], P('comp', None, 'blk'), may hold values from -6 to 6
- adj_source: float32 [4, 6, 256, 128, 128], P('comp', None, 'blk'), may hold values from -6 to 6
- vol_inverse: float32 [4, 256, 128, 128], P('comp', 'blk'), may hold values from 0.5 to 2
- coupling: float32 [4, 6, 6, 6], P('comp'), may hold values from -0.6 to 0.65
- send_tile: int32 [128, 128, 8], P(('comp', 'blk')), may hold values from 0 to 1023
- send_count: int32 [128, 128], P(('comp', 'blk')), may hold values from 0 to 8, as said below
- send_weight: float32 [128, 128, 8], P(('comp', 'blk')), may hold values from 0.2 to 1
- recv_slot: int32 [128, 128, 8], P(('comp', 'blk')), may hold values from 0 to 63
- fringe_row: int32 [128, 64], P(('comp', 'blk')), may hold values from 0 to 1023, as said below
Outputs:
- psi_end: float32 [4, 6, 256, 128, 128], P('comp', None, 'blk')
The draws below stay inside these ranges and needn't reach their ends.
Inputs may be any that keep to these rules, and one draw needn't show every extreme that they name: `send_count`: no tiles travel between devices of the same component; between devices of different components the count is 4 or more. In every draw one receiver gets 8 live entries from every device of the other components. `fringe_row`: the rows of one device's fringe slots are distinct.
All inputs are finite; a program needn't handle non-finite values.
Results may differ from the reference program's by a relative error of at most 0.0003.
Values sent between devices are 32-bit elements; how exact they have to be, the bound alone decides.
No kernel may reach another device: no remote copies, remote signals or barrier semaphores. Data moves between devices by JAX's collectives and lax.ppermute only.
A program may use at most 128 MiB of HBM per device.

```python
import math
import jax
import jax.numpy as jnp
from jax import lax

NVAR = 6
CY = 128
CZ = 128
CAP = 8
SLOTS = 64
COMPS = 4
BLOCKS = 32
PEERS = 128
NX = 256
ROWS = 1024


def draw_coupling(key, part):
    key_diag, key_off = jax.random.split(jax.random.fold_in(key, 5), 2)
    diag = jax.random.uniform(key_diag, (COMPS, 6, NVAR), jnp.float32, 0.35, 0.65)
    off = jnp.clip(jax.random.normal(key_off, (COMPS, 6, NVAR, NVAR), jnp.float32), -5.0, 5.0) * 0.12
    eye = jnp.eye(NVAR, dtype=jnp.float32)
    return off * (1.0 - eye) + diag[..., None] * eye


def draw_send_count(key, part):
    key_base, key_heavy, key_hot = jax.random.split(jax.random.fold_in(key, 11), 3)
    base = jax.random.randint(key_base, (PEERS, PEERS), CAP // 2, CAP + 1)
    heavy = jax.random.randint(key_heavy, (PEERS,), 0, 8) == 0
    hot = jax.random.randint(key_hot, (), 0, PEERS)
    dest = jnp.arange(PEERS, dtype=jnp.int32)[None, :]
    src = jnp.arange(PEERS, dtype=jnp.int32)[:, None]
    full = heavy[None, :] | (dest == hot)
    counts = jnp.where(full, CAP, jnp.minimum(base, CAP))
    same = src // BLOCKS == dest // BLOCKS
    return jnp.where(same, 0, counts).astype(jnp.int32)


def draw_fringe_row(key, part):
    keys = jax.random.split(jax.random.fold_in(key, 3), PEERS)
    picks = jax.vmap(lambda k: jax.random.permutation(k, ROWS)[:SLOTS])(keys)
    return picks.astype(jnp.int32)


def place_ends(drawn, rng, least, largest):
    longest = drawn.shape.index(max(drawn.shape))
    spots = []
    for shift in (0, 1):
        where = [jax.random.randint(jax.random.fold_in(rng, axis), (), 0, length) for axis, length in enumerate(drawn.shape)]
        where[longest] = (where[longest] + shift) % drawn.shape[longest]
        spots.append(tuple(where))
    return drawn.at[spots[0]].set(least).at[spots[1]].set(largest)


def levels(rng, shape, cuts, least, largest):
    factor_of = 1.0
    for position, parts in cuts:
        heights = jax.random.uniform(jax.random.fold_in(jax.random.fold_in(rng, 6), position), (parts,), jnp.float32, least / len(cuts), largest / len(cuts))
        factor_of = factor_of * jnp.repeat(jnp.exp(heights), shape[position] // parts).reshape((-1,) + (1,) * (len(shape) - 1 - position))
    return factor_of


def noise(rng, extent, spread, limit, cuts=(), kind=jnp.bfloat16):
    level = levels(rng, extent, cuts, -0.22, 0.18) if cuts else 1.0
    array = jax.random.normal(rng, extent, jnp.float32) * spread * level
    return jnp.minimum(jnp.maximum(array, -limit), limit).astype(kind)


def setup_inputs(seed: int = 0) -> dict:
    seeds = jax.random.split(jax.random.key(seed), 10)
    return {
        "psi_start": noise(seeds[0], (COMPS, NVAR, NX, CY, CZ), 1.0, 6.0, ((0, 4), (2, 32)), jnp.float32),
        "adj_source": noise(seeds[1], (COMPS, NVAR, NX, CY, CZ), 1.0, 6.0, ((0, 4), (2, 32)), jnp.float32),
        "vol_inverse": jnp.clip(jnp.exp(math.log(2.0) - 1.3862944 * jax.random.uniform(seeds[2], (COMPS, NX, CY, CZ), jnp.float32) ** levels(seeds[2], (COMPS, NX, CY, CZ), ((0, 4), (1, 32)), -0.2, 0.2)), 0.5, 2.0),
        "coupling": draw_coupling(jax.random.fold_in(seeds[9], 71), 0),
        "send_tile": place_ends(jax.random.randint(seeds[4], (PEERS, PEERS, CAP), 0, ROWS), jax.random.fold_in(seeds[4], 1), 0, ROWS - 1).astype(jnp.int32),
        "send_count": draw_send_count(jax.random.fold_in(seeds[9], 71), 0),
        "send_weight": jnp.clip(0.2 + 0.8 * jax.random.uniform(seeds[6], (PEERS, PEERS, CAP), jnp.float32) ** levels(seeds[6], (PEERS, PEERS, CAP), ((0, 128),), -0.2, 0.2), 0.2, 1.0),
        "recv_slot": place_ends(jax.random.randint(seeds[7], (PEERS, PEERS, CAP), 0, SLOTS), jax.random.fold_in(seeds[7], 1), 0, SLOTS - 1).astype(jnp.int32),
        "fringe_row": draw_fringe_row(jax.random.fold_in(seeds[9], 71), 0),
    }


PENALTY = 4.0
TIME_STEP = 0.08


def comp_rate(args):
    field, volume, source, matrices, interp, rows = args
    padded = jnp.pad(field, ((0, 0), (1, 1), (1, 1), (1, 1)))
    diffs = jnp.stack([
        padded[:, 2:, 1:-1, 1:-1] - field,
        padded[:, :-2, 1:-1, 1:-1] - field,
        padded[:, 1:-1, 2:, 1:-1] - field,
        padded[:, 1:-1, :-2, 1:-1] - field,
        padded[:, 1:-1, 1:-1, 2:] - field,
        padded[:, 1:-1, 1:-1, :-2] - field,
    ])
    flux = jnp.einsum('dvu,dvxyz->uxyz', matrices, diffs, precision=lax.Precision.HIGHEST)
    rate = volume[None] * flux + source
    rate4 = rate.reshape(NVAR, BLOCKS, ROWS, CZ)
    field4 = field.reshape(NVAR, BLOCKS, ROWS, CZ)
    block_ids = jnp.arange(BLOCKS, dtype=jnp.int32)[:, None]
    near = field4[:, block_ids, rows, :]
    target = jnp.transpose(interp, (1, 0, 2, 3))
    rate4 = rate4.at[:, block_ids, rows, :].add(PENALTY * (target - near))
    return rate4.reshape(NVAR, NX, CY, CZ)


def fringe_all(field, send_tile, send_count, send_weight, recv_slot):
    tiles = field.reshape(COMPS, NVAR, BLOCKS, ROWS, CZ).transpose(0, 2, 1, 3, 4).reshape(PEERS, NVAR, ROWS, CZ)
    sources = jnp.arange(PEERS, dtype=jnp.int32)[:, None]
    entries = jnp.arange(CAP, dtype=jnp.int32)[None, :]
    slot_ids = jnp.arange(SLOTS, dtype=jnp.int32)[:, None]

    def one(target):
        index = send_tile[:, target, :]
        live = entries < send_count[:, target][:, None]
        weight = jnp.where(live, send_weight[:, target, :], 0.0)
        picked = tiles[sources, :, index, :]
        contrib = (picked * weight[:, :, None, None]).reshape(PEERS * CAP, NVAR, CZ)
        onehot = (recv_slot[target].reshape(1, -1) == slot_ids).astype(jnp.float32)
        return jnp.einsum('sk,kvz->vsz', onehot, contrib, precision=lax.Precision.HIGHEST)

    return lax.map(one, jnp.arange(PEERS, dtype=jnp.int32))


def reference(psi_start, adj_source, vol_inverse, coupling, send_tile, send_count, send_weight, recv_slot, fringe_row):
    rows_comp = fringe_row.reshape(COMPS, BLOCKS, SLOTS)

    def rate_of(field):
        interp = fringe_all(field, send_tile, send_count, send_weight, recv_slot)
        interp_comp = interp.reshape(COMPS, BLOCKS, NVAR, SLOTS, CZ)
        return lax.map(comp_rate, (field, vol_inverse, adj_source, coupling, interp_comp, rows_comp))

    first = rate_of(psi_start)
    middle = psi_start + TIME_STEP * first
    second = rate_of(middle)
    return psi_start + (0.5 * TIME_STEP) * (first + second)
```

```python
import functools

import jax
import jax.numpy as jnp
from jax import lax
from jax.experimental import pallas as pl
from jax.experimental.pallas import tpu as pltpu
from jax.sharding import PartitionSpec as P

PENALTY = 4.0
TIME_STEP = 0.08
NVAR, CX, CY, CZ = 6, 8, 128, 128
ROWS = CX * CY
CAP = 8
SLOTS = 64
PEERS = 128
STEPS = 8
PB = PEERS // STEPS
BAND = 32
MEM = pltpu.MemorySpace


def gather_rows(field, tile, count, weight, out, first):
    def peer_rows(p, carry):
        peer = first + p
        live = count[0, peer]
        for e in range(CAP):
            t = tile[e, peer]
            w = jnp.where(e < live, weight[e, peer], 0.0)
            for v in range(NVAR):
                out[p, pl.ds(v * CAP + e, 1), :] = field[v, pl.ds(t, 1), :] * w
        return carry

    lax.fori_loop(0, PB, peer_rows, 0)


def reduce_rows(slots, arrived, total):
    slot_ids = lax.broadcasted_iota(jnp.int32, (SLOTS, PB * CAP), 0)
    onehot = (slots[...] == slot_ids).astype(jnp.bfloat16)
    for v in range(NVAR):
        part = arrived[:, v * CAP : (v + 1) * CAP, :].reshape(PB * CAP, CZ)
        high = part.astype(jnp.bfloat16)
        low = (part - high.astype(jnp.float32)).astype(jnp.bfloat16)
        both = jnp.dot(onehot, jnp.concatenate([high, low], axis=1), preferred_element_type=jnp.float32)
        total[v] += both[:, :CZ] + both[:, CZ:]


def send_kernel(tile, count, weight, field, out):
    gather_rows(field, tile, count, weight, out, pl.program_id(0) * PB)


def middle_kernel(tile, count, weight, rows, slots, arrived, start_mid, sent, mid, field, total, sems):
    step = pl.program_id(0)
    load = pltpu.make_async_copy(start_mid, field, sems.at[0])
    store = pltpu.make_async_copy(field, mid, sems.at[1])

    @pl.when(step == 0)
    def _():
        load.start()
        total[...] = jnp.zeros_like(total)

    @pl.when(step < STEPS)
    def _():
        reduce_rows(slots, arrived, total)

    @pl.when(step == STEPS - 1)
    def _():
        load.wait()

        def patch(s, carry):
            t = rows[0, s]
            for v in range(NVAR):
                field[v, pl.ds(t, 1), :] += (TIME_STEP * PENALTY) * total[v, pl.ds(s, 1), :]
            return carry

        lax.fori_loop(0, SLOTS, patch, 0)
        store.start()

    @pl.when(step >= STEPS)
    def _():
        gather_rows(field, tile, count, weight, sent, (step - STEPS) * PB)

    @pl.when(step == 2 * STEPS - 1)
    def _():
        store.wait()


def last_kernel(rows, slots, arrived, start_end, end, field, total, sems):
    step = pl.program_id(0)
    load = pltpu.make_async_copy(start_end, field, sems.at[0])
    store = pltpu.make_async_copy(field, end, sems.at[1])

    @pl.when(step == 0)
    def _():
        load.start()
        total[...] = jnp.zeros_like(total)

    reduce_rows(slots, arrived, total)

    @pl.when(step == STEPS - 1)
    def _():
        load.wait()

        def patch(s, carry):
            t = rows[0, s]
            for v in range(NVAR):
                field[v, pl.ds(t, 1), :] += (0.5 * TIME_STEP * PENALTY) * total[v, pl.ds(s, 1), :]
            return carry

        lax.fori_loop(0, SLOTS, patch, 0)
        store.start()
        store.wait()


def flux_kernel(second, coupling, rows, below, above, *refs):
    if second:
        field, base, source, volume, out, ext, sems = refs
    else:
        field, source, volume, out, ext, sems = refs
    x = pl.program_id(0)
    body = pltpu.make_async_copy(field, ext.at[:, pl.ds(1, CX), pl.ds(8, CY), :], sems.at[0])
    low = pltpu.make_async_copy(below, ext.at[:, 0, pl.ds(8, CY), :], sems.at[1])
    high = pltpu.make_async_copy(above, ext.at[:, CX + 1, pl.ds(8, CY), :], sems.at[2])

    @pl.when(x == 0)
    def _():
        body.start()
        low.start()
        high.start()
        edge = jnp.zeros((NVAR, CX + 2, 8, CZ), jnp.float32)
        ext[:, :, 0:8, :] = edge
        ext[:, :, 8 + CY : 16 + CY, :] = edge
        body.wait()
        low.wait()
        high.wait()

    lane = lax.broadcasted_iota(jnp.int32, (BAND, CZ), 1)

    def band(i, carry):
        y = pl.multiple_of(i * BAND, BAND)
        flux = [jnp.zeros((BAND, CZ), jnp.float32) for _ in range(NVAR)]
        for w in range(NVAR):
            center = ext[w, x + 1, pl.ds(y + 8, BAND), :]
            for d in range(6):
                if d == 0:
                    near = ext[w, x + 2, pl.ds(y + 8, BAND), :]
                elif d == 1:
                    near = ext[w, x, pl.ds(y + 8, BAND), :]
                elif d == 2:
                    near = ext[w, x + 1, pl.ds(y + 9, BAND), :]
                elif d == 3:
                    near = ext[w, x + 1, pl.ds(y + 7, BAND), :]
                elif d == 4:
                    near = jnp.where(lane == CZ - 1, 0.0, pltpu.roll(center, CZ - 1, 1))
                else:
                    near = jnp.where(lane == 0, 0.0, pltpu.roll(center, 1, 1))
                diff = near - center
                for u in range(NVAR):
                    flux[u] = flux[u] + coupling[d, w * NVAR + u] * diff
        vol = volume[0, pl.ds(y, BAND), :]
        for u in range(NVAR):
            rate = vol * flux[u] + source[u, 0, pl.ds(y, BAND), :]
            center = ext[u, x + 1, pl.ds(y + 8, BAND), :]
            if second:
                value = 0.5 * (base[u, 0, pl.ds(y, BAND), :] + center) + (0.5 * TIME_STEP) * rate
            else:
                value = center + TIME_STEP * rate
            out[u, x, pl.ds(y, BAND), :] = value
        return carry

    lax.fori_loop(0, CY // BAND, band, 0)

    @pl.when(x == CX - 1)
    def _():
        scale = PENALTY * TIME_STEP * (0.5 if second else 1.0)

        def patch(s, carry):
            t = rows[0, s]
            a, b = t // CY, t % CY
            for v in range(NVAR):
                out[v, a, pl.ds(b, 1), :] -= scale * ext[v, a + 1, pl.ds(b + 8, 1), :]
            return carry

        lax.fori_loop(0, SLOTS, patch, 0)


SMEM = pl.BlockSpec(memory_space=MEM.SMEM)
ANY = pl.BlockSpec(memory_space=pl.ANY)
FIELD = jax.ShapeDtypeStruct((NVAR, CX, CY, CZ), jnp.float32)
FLAT = jax.ShapeDtypeStruct((NVAR, ROWS, CZ), jnp.float32)
SENT = jax.ShapeDtypeStruct((PEERS, NVAR * CAP, CZ), jnp.float32)


def params(mib):
    return pltpu.CompilerParams(dimension_semantics=("arbitrary",), vmem_limit_bytes=mib << 20)


def pack(field, tile, count, weight):
    return pl.pallas_call(
        send_kernel,
        grid=(STEPS,),
        in_specs=[SMEM, SMEM, SMEM, pl.BlockSpec((NVAR, ROWS, CZ), lambda i: (0, 0, 0))],
        out_specs=pl.BlockSpec((PB, NVAR * CAP, CZ), lambda i: (i, 0, 0)),
        out_shape=SENT,
        compiler_params=params(24),
        cost_estimate=pl.CostEstimate(flops=10**6, bytes_accessed=7 << 20, transcendentals=0),
        name="pack",
    )(tile, count, weight, field)


def middle(arrived, mid, tile, count, weight, rows, slots):
    last = STEPS - 1
    return pl.pallas_call(
        middle_kernel,
        grid=(2 * STEPS,),
        in_specs=[
            SMEM,
            SMEM,
            SMEM,
            SMEM,
            pl.BlockSpec((1, PB * CAP), lambda i: (0, jnp.minimum(i, last))),
            pl.BlockSpec((PB, NVAR * CAP, CZ), lambda i: (jnp.minimum(i, last), 0, 0)),
            ANY,
        ],
        out_specs=[pl.BlockSpec((PB, NVAR * CAP, CZ), lambda i: (jnp.maximum(i - STEPS, 0), 0, 0)), ANY],
        out_shape=[SENT, FLAT],
        scratch_shapes=[
            pltpu.VMEM((NVAR, ROWS, CZ), jnp.float32),
            pltpu.VMEM((NVAR, SLOTS, CZ), jnp.float32),
            pltpu.SemaphoreType.DMA((2,)),
        ],
        compiler_params=params(24),
        cost_estimate=pl.CostEstimate(flops=10**8, bytes_accessed=12 << 20, transcendentals=0),
        name="middle",
    )(tile, count, weight, rows, slots, arrived, mid)


def finish(arrived, end, rows, slots):
    return pl.pallas_call(
        last_kernel,
        grid=(STEPS,),
        in_specs=[
            SMEM,
            pl.BlockSpec((1, PB * CAP), lambda i: (0, i)),
            pl.BlockSpec((PB, NVAR * CAP, CZ), lambda i: (i, 0, 0)),
            ANY,
        ],
        out_specs=ANY,
        out_shape=FLAT,
        scratch_shapes=[
            pltpu.VMEM((NVAR, ROWS, CZ), jnp.float32),
            pltpu.VMEM((NVAR, SLOTS, CZ), jnp.float32),
            pltpu.SemaphoreType.DMA((2,)),
        ],
        compiler_params=params(24),
        cost_estimate=pl.CostEstimate(flops=10**8, bytes_accessed=9 << 20, transcendentals=0),
        name="finish",
    )(rows, slots, arrived, end)


def advance(second, coupling, rows, below, above, field, base, source, volume):
    plane = pl.BlockSpec((NVAR, 1, CY, CZ), lambda i: (0, i, 0, 0))
    fields = [field, base, source] if second else [field, source]
    return pl.pallas_call(
        functools.partial(flux_kernel, second),
        grid=(CX,),
        in_specs=[SMEM, SMEM, ANY, ANY, ANY]
        + [plane] * (len(fields) - 1)
        + [pl.BlockSpec((1, CY, CZ), lambda i: (i, 0, 0))],
        out_specs=pl.BlockSpec((NVAR, CX, CY, CZ), lambda i: (0, 0, 0, 0)),
        out_shape=FIELD,
        scratch_shapes=[
            pltpu.VMEM((NVAR, CX + 2, CY + 16, CZ), jnp.float32),
            pltpu.SemaphoreType.DMA((3,)),
        ],
        compiler_params=params(40),
        cost_estimate=pl.CostEstimate(flops=60 * 10**6, bytes_accessed=12 << 20, transcendentals=0),
        name="advance",
    )(coupling, rows, below, above, *fields, volume)


def halos(field):
    count = lax.axis_size("blk")
    below = lax.ppermute(field[:, -1], "blk", [(i, i + 1) for i in range(count - 1)])
    above = lax.ppermute(field[:, 0], "blk", [(i + 1, i) for i in range(count - 1)])
    return below, above


def exchange(sent):
    return lax.all_to_all(sent, ("comp", "blk"), split_axis=0, concat_axis=0, tiled=True)


def shards(psi_start, adj_source, vol_inverse, coupling, send_tile, send_count, send_weight, recv_slot, fringe_row):
    start = psi_start[0]
    source = adj_source[0]
    volume = vol_inverse[0]
    matrices = coupling[0].reshape(6, NVAR * NVAR)
    tile = send_tile[0].T
    weight = send_weight[0].T
    slots = recv_slot[0].reshape(1, PEERS * CAP)

    sent = pack(start.reshape(NVAR, ROWS, CZ), tile, send_count, weight)
    arrived = exchange(sent)
    below, above = halos(start)
    mid = advance(False, matrices, fringe_row, below, above, start, None, source, volume)
    sent, mid = middle(arrived, mid.reshape(NVAR, ROWS, CZ), tile, send_count, weight, fringe_row, slots)
    arrived = exchange(sent)
    mid = mid.reshape(NVAR, CX, CY, CZ)
    below, above = halos(mid)
    end = advance(True, matrices, fringe_row, below, above, mid, start, source, volume)
    end = finish(arrived, end.reshape(NVAR, ROWS, CZ), fringe_row, slots)
    return end.reshape(1, NVAR, CX, CY, CZ)


def solution(mesh):
    in_specs = (
        P("comp", None, "blk", None, None),
        P("comp", None, "blk", None, None),
        P("comp", "blk", None, None),
        P("comp", None, None, None),
        P(("comp", "blk"), None, None),
        P(("comp", "blk"), None),
        P(("comp", "blk"), None, None),
        P(("comp", "blk"), None, None),
        P(("comp", "blk"), None),
    )
    out_specs = P("comp", None, "blk", None, None)
    return jax.shard_map(shards, mesh=mesh, in_specs=in_specs, out_specs=out_specs, check_vma=False)
```

```python
import functools

import jax
import jax.numpy as jnp
from jax import lax
from jax.experimental import pallas as pl
from jax.experimental.pallas import tpu as pltpu
from jax.sharding import PartitionSpec as P

PENALTY = 4.0
TIME_STEP = 0.08
NVAR, CX, CY, CZ = 6, 8, 128, 128
ROWS = CX * CY
CAP = 8
SLOTS = 64
COMPS = 4
BLOCKS = 32
PEERS = COMPS * BLOCKS
OTHERS = COMPS - 1
PACK = NVAR * CAP
BAND = 32
F32 = jnp.float32
HBM = pl.BlockSpec(memory_space=pltpu.HBM)
SMEM = pl.BlockSpec(memory_space=pltpu.SMEM)
ANY = pl.BlockSpec(memory_space=pl.ANY)
DMA = pltpu.SemaphoreType.DMA


def shape(*dims):
    return jax.ShapeDtypeStruct(dims, F32)


def start_all(copies):
    for copy in copies:
        copy.start()


def wait_all(copies):
    for copy in copies:
        copy.wait()


def other(j):
    return lax.rem(lax.axis_index("comp") + j + 1, COMPS)


def block_of(ref, j):
    return ref.at[pl.ds(other(j) * BLOCKS, BLOCKS)]


def part_of(ref, j):
    return ref.at[pl.ds(j * BLOCKS, BLOCKS)]


def table_copies(tables, scratch, sems):
    return [pltpu.make_async_copy(a, b, sems.at[i]) for i, (a, b) in enumerate(zip(tables, scratch))]


def gather_rows(field, tables, buf, sent, sems):
    tile, count, weight = tables
    stores = []
    for j in range(OTHERS):
        first = other(j) * BLOCKS

        def peer_rows(b, carry):
            peer = first + b
            live = count[0, peer]
            for e in range(CAP):
                t = tile[e, peer]
                w = jnp.where(e < live, weight[e, peer], 0.0)
                for v in range(NVAR):
                    buf[j * BLOCKS + b, pl.ds(v * CAP + e, 1), :] = field[v, pl.ds(t, 1), :] * w
            return carry

        lax.fori_loop(0, BLOCKS, peer_rows, 0)
        stores.append(pltpu.make_async_copy(part_of(buf, j), block_of(sent, j), sems.at[j]))
        stores[-1].start()
    return stores


def reduce_rows(slots, loads, data, total):
    slot_ids = lax.broadcasted_iota(jnp.int32, (SLOTS, BLOCKS * CAP), 0)
    for j in range(OTHERS):
        onehot = (slots[pl.ds(other(j), 1), :] == slot_ids).astype(F32).astype(jnp.bfloat16)
        loads[j].wait()
        for v in range(NVAR):
            part = data[j * BLOCKS : (j + 1) * BLOCKS, v * CAP : (v + 1) * CAP, :].reshape(BLOCKS * CAP, CZ)
            high = part.astype(jnp.bfloat16)
            low = (part - high.astype(F32)).astype(jnp.bfloat16)
            both = jnp.dot(onehot, jnp.concatenate([high, low], axis=1), preferred_element_type=F32)
            both = both[:, :CZ] + both[:, CZ:]
            total[v] = both if j == 0 else total[v] + both


def add_halos(field, coupling, below, above, volume, scale):
    for side, halo, first in ((1, below, 0), (0, above, ROWS - CY)):

        def band(i, carry):
            y = pl.multiple_of(i * BAND, BAND)
            vol = volume[1 - side, pl.ds(y, BAND), :] * scale
            near = [halo[w, pl.ds(y, BAND), :] for w in range(NVAR)]
            for u in range(NVAR):
                flux = coupling[side, u] * near[0]
                for w in range(1, NVAR):
                    flux = flux + coupling[side, w * NVAR + u] * near[w]
                field[u, pl.ds(first + y, BAND), :] += vol * flux
            return carry

        lax.fori_loop(0, CY // BAND, band, 0)


def patch_rows(field, rows, total, scale):
    def patch(s, carry):
        t = rows[0, s]
        for v in range(NVAR):
            field[v, pl.ds(t, 1), :] += scale * total[v, pl.ds(s, 1), :]
        return carry

    lax.fori_loop(0, SLOTS, patch, 0)


def pack_kernel(tile, count, weight, field, sent, tile_s, count_s, weight_s, field_v, buf, sems, sent_sems):
    scratch = (tile_s, count_s, weight_s)
    copies = table_copies((tile, count, weight), scratch, sems)
    copies.append(pltpu.make_async_copy(field, field_v, sems.at[3]))
    start_all(copies)
    wait_all(copies)
    wait_all(gather_rows(field_v, scratch, buf, sent, sent_sems))


def arrive(slots, arrived, guess, below, above, volume, data, total, field, below_v, above_v, volume_v, sems):
    copies = [
        pltpu.make_async_copy(guess, field, sems.at[3]),
        pltpu.make_async_copy(below, below_v, sems.at[4]),
        pltpu.make_async_copy(above, above_v, sems.at[5]),
        pltpu.make_async_copy(volume.at[0], volume_v.at[0], sems.at[6]),
        pltpu.make_async_copy(volume.at[CX - 1], volume_v.at[1], sems.at[7]),
    ]
    loads = [pltpu.make_async_copy(block_of(arrived, j), part_of(data, j), sems.at[j]) for j in range(OTHERS)]
    start_all(loads + copies)
    reduce_rows(slots, loads, data, total)
    wait_all(copies)


def middle_kernel(
    coupling, rows, slots, tile, count, weight, arrived, guess, below, above, volume,
    sent, mid, low, high,
    tile_s, count_s, weight_s, data, total, field, below_v, above_v, volume_v, sems, table_sems, sent_sems,
):
    scratch = (tile_s, count_s, weight_s)
    tables = table_copies((tile, count, weight), scratch, table_sems)
    start_all(tables)
    arrive(slots, arrived, guess, below, above, volume, data, total, field, below_v, above_v, volume_v, sems)
    add_halos(field, coupling, below_v, above_v, volume_v, TIME_STEP)
    patch_rows(field, rows, total, TIME_STEP * PENALTY)
    stores = [
        pltpu.make_async_copy(field.at[:, pl.ds(0, CY), :], low, sems.at[0]),
        pltpu.make_async_copy(field.at[:, pl.ds(ROWS - CY, CY), :], high, sems.at[1]),
        pltpu.make_async_copy(field, mid, sems.at[2]),
    ]
    start_all(stores)
    wait_all(tables)
    wait_all(gather_rows(field, scratch, data, sent, sent_sems))
    wait_all(stores)


def finish_kernel(
    coupling, rows, slots, arrived, guess, below, above, volume,
    end,
    data, total, field, below_v, above_v, volume_v, sems,
):
    arrive(slots, arrived, guess, below, above, volume, data, total, field, below_v, above_v, volume_v, sems)
    add_halos(field, coupling, below_v, above_v, volume_v, 0.5 * TIME_STEP)
    patch_rows(field, rows, total, 0.5 * TIME_STEP * PENALTY)
    stores = [pltpu.make_async_copy(field.at[v], end.at[v], sems.at[v]) for v in range(NVAR)]
    start_all(stores)
    wait_all(stores)


def flux_kernel(second, coupling, rows, field, *refs):
    if second:
        base, source, volume, out, ext, sem = refs
    else:
        source, volume, out, ext, sem = refs
    x = pl.program_id(0)

    @pl.when(x == 0)
    def _():
        copy = pltpu.make_async_copy(field, ext.at[:, pl.ds(1, CX), pl.ds(8, CY), :], sem)
        copy.start()
        edge = jnp.zeros((NVAR, CX + 2, 8, CZ), F32)
        ext[:, :, 0:8, :] = edge
        ext[:, :, 8 + CY : 16 + CY, :] = edge
        plane = jnp.zeros((NVAR, CY, CZ), F32)
        ext[:, 0, 8 : 8 + CY, :] = plane
        ext[:, CX + 1, 8 : 8 + CY, :] = plane
        copy.wait()

    lane = lax.broadcasted_iota(jnp.int32, (BAND, CZ), 1)

    def band(i, carry):
        y = pl.multiple_of(i * BAND, BAND)
        flux = [jnp.zeros((BAND, CZ), F32) for _ in range(NVAR)]
        for w in range(NVAR):
            center = ext[w, x + 1, pl.ds(y + 8, BAND), :]
            for d in range(6):
                if d == 0:
                    near = ext[w, x + 2, pl.ds(y + 8, BAND), :]
                elif d == 1:
                    near = ext[w, x, pl.ds(y + 8, BAND), :]
                elif d == 2:
                    near = ext[w, x + 1, pl.ds(y + 9, BAND), :]
                elif d == 3:
                    near = ext[w, x + 1, pl.ds(y + 7, BAND), :]
                elif d == 4:
                    near = jnp.where(lane == CZ - 1, 0.0, pltpu.roll(center, CZ - 1, 1))
                else:
                    near = jnp.where(lane == 0, 0.0, pltpu.roll(center, 1, 1))
                diff = near - center
                for u in range(NVAR):
                    flux[u] = flux[u] + coupling[d, w * NVAR + u] * diff
        vol = volume[0, pl.ds(y, BAND), :]
        for u in range(NVAR):
            rate = vol * flux[u] + source[u, 0, pl.ds(y, BAND), :]
            center = ext[u, x + 1, pl.ds(y + 8, BAND), :]
            if second:
                value = 0.5 * (base[u, 0, pl.ds(y, BAND), :] + center) + (0.5 * TIME_STEP) * rate
            else:
                value = center + TIME_STEP * rate
            out[u, x, pl.ds(y, BAND), :] = value
        return carry

    lax.fori_loop(0, CY // BAND, band, 0)

    @pl.when(x == CX - 1)
    def _():
        scale = PENALTY * TIME_STEP * (0.5 if second else 1.0)

        def patch(s, carry):
            t = rows[0, s]
            a, b = t // CY, t % CY
            for v in range(NVAR):
                out[v, a, pl.ds(b, 1), :] -= scale * ext[v, a + 1, pl.ds(b + 8, 1), :]
            return carry

        lax.fori_loop(0, SLOTS, patch, 0)


TABLES = [
    pltpu.SMEM((CAP, PEERS), jnp.int32),
    pltpu.SMEM((1, PEERS), jnp.int32),
    pltpu.SMEM((CAP, PEERS), F32),
]
FIELD_V = pltpu.VMEM((NVAR, ROWS, CZ), F32)
DATA_V = pltpu.VMEM((OTHERS * BLOCKS, PACK, CZ), F32)
ARRIVE = [
    DATA_V,
    pltpu.VMEM((NVAR, SLOTS, CZ), F32),
    FIELD_V,
    pltpu.VMEM((NVAR, CY, CZ), F32),
    pltpu.VMEM((NVAR, CY, CZ), F32),
    pltpu.VMEM((2, CY, CZ), F32),
    DMA((8,)),
]
SLOT_ROWS = pl.BlockSpec((COMPS, BLOCKS * CAP), lambda: (0, 0))


def call(kernel, name, specs, inputs, out_shape, scratch, moved, flops):
    single = not isinstance(out_shape, list)
    return pl.pallas_call(
        kernel,
        in_specs=specs,
        out_specs=HBM if single else [HBM] * len(out_shape),
        out_shape=out_shape,
        scratch_shapes=scratch,
        compiler_params=pltpu.CompilerParams(vmem_limit_bytes=60 << 20),
        cost_estimate=pl.CostEstimate(flops=flops, bytes_accessed=moved, transcendentals=0),
        name=name,
    )(*inputs)


def pack(tables, field):
    return call(
        pack_kernel, "pack", [HBM] * 4, [*tables, field], shape(PEERS, PACK, CZ),
        [*TABLES, FIELD_V, DATA_V, DMA((4,)), DMA((OTHERS,))], 8 << 20, 10**6,
    )


def middle(matrices, rows, slots, tables, arrived, mid, below, above, volume):
    return call(
        middle_kernel, "middle", [SMEM, SMEM, SLOT_ROWS, HBM, HBM, HBM, ANY, HBM, ANY, ANY, HBM],
        [matrices, rows, slots, *tables, arrived, mid, below, above, volume],
        [shape(PEERS, PACK, CZ), shape(NVAR, ROWS, CZ), shape(NVAR, CY, CZ), shape(NVAR, CY, CZ)],
        [*TABLES, *ARRIVE, DMA((3,)), DMA((OTHERS,))], 16 << 20, 10**8,
    )


def finish(matrices, rows, slots, arrived, end, below, above, volume):
    return call(
        finish_kernel, "finish", [SMEM, SMEM, SLOT_ROWS, ANY, HBM, ANY, ANY, HBM],
        [matrices, rows, slots, arrived, end, below, above, volume],
        shape(NVAR, ROWS, CZ), ARRIVE, 10 << 20, 10**8,
    )


def advance(second, coupling, rows, field, streams, volume):
    return pl.pallas_call(
        functools.partial(flux_kernel, second),
        grid=(CX,),
        in_specs=[SMEM, SMEM, HBM]
        + [pl.BlockSpec((NVAR, 1, CY, CZ), lambda i: (0, i, 0, 0))] * len(streams)
        + [pl.BlockSpec((1, CY, CZ), lambda i: (i, 0, 0))],
        out_specs=pl.BlockSpec((NVAR, CX, CY, CZ), lambda i: (0, 0, 0, 0)),
        out_shape=shape(NVAR, CX, CY, CZ),
        scratch_shapes=[pltpu.VMEM((NVAR, CX + 2, CY + 16, CZ), F32), DMA(())],
        compiler_params=pltpu.CompilerParams(dimension_semantics=("arbitrary",), vmem_limit_bytes=60 << 20),
        cost_estimate=pl.CostEstimate(flops=60 * 10**6, bytes_accessed=40 << 20, transcendentals=0),
        name="advance_end" if second else "advance_mid",
    )(coupling, rows, field, *streams, volume)


def exchange(sent):
    return lax.all_to_all(sent, ("comp", "blk"), split_axis=0, concat_axis=0, tiled=True)


def halos(low, high):
    count = lax.axis_size("blk")
    below = lax.ppermute(high, "blk", [(i, i + 1) for i in range(count - 1)])
    above = lax.ppermute(low, "blk", [(i + 1, i) for i in range(count - 1)])
    return below, above


def shards(psi_start, adj_source, vol_inverse, coupling, send_tile, send_count, send_weight, recv_slot, fringe_row):
    start = psi_start[0]
    source = adj_source[0]
    volume = vol_inverse[0]
    matrices = coupling[0].reshape(6, NVAR * NVAR)
    tables = [send_tile[0].T, send_count, send_weight[0].T]
    slots = recv_slot[0].reshape(COMPS, BLOCKS * CAP)

    arrived = exchange(pack(tables, start.reshape(NVAR, ROWS, CZ)))
    below, above = halos(start[:, 0], start[:, -1])
    mid = advance(False, matrices, fringe_row, start, [source], volume).reshape(NVAR, ROWS, CZ)
    sent, mid, low, high = middle(matrices, fringe_row, slots, tables, arrived, mid, below, above, volume)
    arrived = exchange(sent)
    below, above = halos(low, high)
    end = advance(True, matrices, fringe_row, mid.reshape(NVAR, CX, CY, CZ), [start, source], volume)
    end = finish(matrices, fringe_row, slots, arrived, end.reshape(NVAR, ROWS, CZ), below, above, volume)
    return end.reshape(1, NVAR, CX, CY, CZ)


def solution(mesh):
    in_specs = (
        P("comp", None, "blk", None, None),
        P("comp", None, "blk", None, None),
        P("comp", "blk", None, None),
        P("comp", None, None, None),
        P(("comp", "blk"), None, None),
        P(("comp", "blk"), None),
        P(("comp", "blk"), None, None),
        P(("comp", "blk"), None, None),
        P(("comp", "blk"), None),
    )
    out_specs = P("comp", None, "blk", None, None)
    return jax.shard_map(shards, mesh=mesh, in_specs=in_specs, out_specs=out_specs, check_vma=False)
```

```python
import functools

import jax
import jax.numpy as jnp
from jax import lax
from jax.experimental import pallas as pl
from jax.experimental.pallas import tpu as pltpu
from jax.sharding import PartitionSpec as P

PENALTY = 4.0
TIME_STEP = 0.08
NVAR, CX, CY, CZ = 6, 8, 128, 128
ROWS = CX * CY
CAP = 8
SLOTS = 64
COMPS = 4
BLOCKS = 32
PEERS = COMPS * BLOCKS
OTHERS = COMPS - 1
PACK = NVAR * CAP
BAND = 32
EDGE = 8
VMEM_LIMIT = 67_000_000
F32 = jnp.float32
HBM = pl.BlockSpec(memory_space=pltpu.HBM)
SMEM = pl.BlockSpec(memory_space=pltpu.SMEM)
DMA = pltpu.SemaphoreType.DMA


def shape(*dims):
    return jax.ShapeDtypeStruct(dims, F32)


def start_all(copies):
    for copy in copies:
        copy.start()


def wait_all(copies):
    for copy in copies:
        copy.wait()


def other(j):
    return lax.rem(lax.axis_index("comp") + j + 1, COMPS)


def block_of(ref, j):
    return ref.at[pl.ds(other(j) * BLOCKS, BLOCKS)]


def part_of(ref, j):
    return ref.at[pl.ds(j * BLOCKS, BLOCKS)]


def gather_rows(field, tables, buf, sent, sems):
    tile, count, weight = tables
    row_ids = lax.broadcasted_iota(jnp.int32, (CAP, CZ), 0)
    stores = []
    for j in range(OTHERS):
        first = other(j) * BLOCKS

        def peer_rows(b, carry):
            peer = first + b
            live = count[0, peer]
            spots = [tile[e, peer] + (EDGE - e) for e in range(CAP)]
            scale = jnp.full((CAP, CZ), weight[0, peer])
            for e in range(1, CAP):
                scale = jnp.where(row_ids == e, weight[e, peer], scale)
            scale = jnp.where(row_ids < live, scale, 0.0)
            for v in range(NVAR):
                rows = field[v, pl.ds(spots[0], CAP), :]
                for e in range(1, CAP):
                    rows = jnp.where(row_ids == e, field[v, pl.ds(spots[e], CAP), :], rows)
                buf[j * BLOCKS + b, v * CAP : (v + 1) * CAP, :] = rows * scale
            return carry

        lax.fori_loop(0, BLOCKS, peer_rows, 0)
        stores.append(pltpu.make_async_copy(part_of(buf, j), block_of(sent, j), sems.at[j]))
        stores[-1].start()
    return stores


def reduce_rows(slots, loads, data, total):
    slot_ids = lax.broadcasted_iota(jnp.int32, (SLOTS, BLOCKS * CAP), 0)
    for j in range(OTHERS):
        onehot = (slots[pl.ds(other(j), 1), :] == slot_ids).astype(F32).astype(jnp.bfloat16)
        loads[j].wait()
        for v in range(NVAR):
            part = data[j * BLOCKS : (j + 1) * BLOCKS, v * CAP : (v + 1) * CAP, :].reshape(BLOCKS * CAP, CZ)
            high = part.astype(jnp.bfloat16)
            low = (part - high.astype(F32)).astype(jnp.bfloat16)
            both = jnp.dot(onehot, jnp.concatenate([high, low], axis=1), preferred_element_type=F32)
            both = both[:, :CZ] + both[:, CZ:]
            total[v] = both if j == 0 else total[v] + both


def add_halos(field, coupling, below, above, volume, scale):
    for side, halo, first in ((1, below, EDGE), (0, above, EDGE + ROWS - CY)):

        def band(i, carry):
            y = pl.multiple_of(i * BAND, BAND)
            vol = volume[1 - side, pl.ds(y, BAND), :] * scale
            near = [halo[w, pl.ds(y, BAND), :] for w in range(NVAR)]
            for u in range(NVAR):
                flux = coupling[side, u] * near[0]
                for w in range(1, NVAR):
                    flux = flux + coupling[side, w * NVAR + u] * near[w]
                field[u, pl.ds(first + y, BAND), :] += vol * flux
            return carry

        lax.fori_loop(0, CY // BAND, band, 0)


def patch_rows(field, rows, total, scale):
    def patch(s, carry):
        t = rows[0, s] + EDGE
        for v in range(NVAR):
            field[v, pl.ds(t, 1), :] += scale * total[v, pl.ds(s, 1), :]
        return carry

    lax.fori_loop(0, SLOTS, patch, 0)


def inner(field, first=0, size=ROWS):
    return field.at[:, pl.ds(EDGE + first, size), :]


def copies_of(pairs, sems, first=0):
    return [pltpu.make_async_copy(a, b, sems.at[first + i]) for i, (a, b) in enumerate(pairs)]


def pack_kernel(tile, count, weight, field, sent, tile_s, count_s, weight_s, field_v, buf, sems, sent_sems):
    scratch = (tile_s, count_s, weight_s)
    pairs = list(zip((tile, count, weight), scratch)) + [(field, inner(field_v))]
    copies = copies_of(pairs, sems)
    start_all(copies)
    wait_all(copies)
    wait_all(gather_rows(field_v, scratch, buf, sent, sent_sems))


def arrive(inputs, scratch, sems):
    coupling, rows, slots, arrived, guess, below, above, volume = inputs
    coupling_s, rows_s, slots_v, data, total, field, below_v, above_v, volume_v = scratch
    loads = [(slots, slots_v)] + [(block_of(arrived, j), part_of(data, j)) for j in range(OTHERS)]
    others = [(guess, inner(field)), (coupling, coupling_s), (rows, rows_s), (below, below_v), (above, above_v)]
    others += [(volume.at[0], volume_v.at[0]), (volume.at[CX - 1], volume_v.at[1])]
    loads = copies_of(loads, sems)
    others = copies_of(others, sems, len(loads))
    start_all(loads + others)
    loads[0].wait()
    reduce_rows(slots_v, loads[1:], data, total)
    wait_all(others)


def middle_kernel(*refs):
    tables, inputs, refs = refs[:3], refs[3:11], refs[11:]
    sent, mid, low, high, refs = *refs[:4], refs[4:]
    table_scratch, scratch, (sems, table_sems, sent_sems) = refs[:3], refs[3:12], refs[12:]
    coupling, rows, _, data, total, field, below, above, volume = scratch
    table_copies = copies_of(list(zip(tables, table_scratch)), table_sems)
    start_all(table_copies)
    arrive(inputs, scratch, sems)
    add_halos(field, coupling, below, above, volume, TIME_STEP)
    patch_rows(field, rows, total, TIME_STEP * PENALTY)
    stores = copies_of([(inner(field), mid), (inner(field, 0, CY), low), (inner(field, ROWS - CY, CY), high)], sems)
    start_all(stores)
    wait_all(table_copies)
    wait_all(gather_rows(field, table_scratch, data, sent, sent_sems))
    wait_all(stores)


def finish_kernel(*refs):
    inputs, end, scratch, sems = refs[:8], refs[8], refs[9:18], refs[18]
    coupling, rows, _, _, total, field, below, above, volume = scratch
    arrive(inputs, scratch, sems)
    add_halos(field, coupling, below, above, volume, 0.5 * TIME_STEP)
    patch_rows(field, rows, total, 0.5 * TIME_STEP * PENALTY)
    stores = copies_of([(inner(field), end)], sems)
    start_all(stores)
    wait_all(stores)


def flux_kernel(second, coupling, rows, field, *refs):
    if second:
        base, source, volume, out, ext, sem = refs
    else:
        source, volume, out, ext, sem = refs
    x = pl.program_id(0)

    @pl.when(x == 0)
    def _():
        copy = pltpu.make_async_copy(field, ext.at[:, pl.ds(1, CX), pl.ds(8, CY), :], sem)
        copy.start()
        edge = jnp.zeros((NVAR, CX + 2, 8, CZ), F32)
        ext[:, :, 0:8, :] = edge
        ext[:, :, 8 + CY : 16 + CY, :] = edge
        plane = jnp.zeros((NVAR, CY, CZ), F32)
        ext[:, 0, 8 : 8 + CY, :] = plane
        ext[:, CX + 1, 8 : 8 + CY, :] = plane
        copy.wait()

    lane = lax.broadcasted_iota(jnp.int32, (BAND, CZ), 1)

    def band(i, carry):
        y = pl.multiple_of(i * BAND, BAND)
        flux = [jnp.zeros((BAND, CZ), F32) for _ in range(NVAR)]
        for w in range(NVAR):
            center = ext[w, x + 1, pl.ds(y + 8, BAND), :]
            for d in range(6):
                if d == 0:
                    near = ext[w, x + 2, pl.ds(y + 8, BAND), :]
                elif d == 1:
                    near = ext[w, x, pl.ds(y + 8, BAND), :]
                elif d == 2:
                    near = ext[w, x + 1, pl.ds(y + 9, BAND), :]
                elif d == 3:
                    near = ext[w, x + 1, pl.ds(y + 7, BAND), :]
                elif d == 4:
                    near = jnp.where(lane == CZ - 1, 0.0, pltpu.roll(center, CZ - 1, 1))
                else:
                    near = jnp.where(lane == 0, 0.0, pltpu.roll(center, 1, 1))
                diff = near - center
                for u in range(NVAR):
                    flux[u] = flux[u] + coupling[d, w * NVAR + u] * diff
        vol = volume[0, pl.ds(y, BAND), :]
        for u in range(NVAR):
            rate = vol * flux[u] + source[u, 0, pl.ds(y, BAND), :]
            center = ext[u, x + 1, pl.ds(y + 8, BAND), :]
            if second:
                value = 0.5 * (base[u, 0, pl.ds(y, BAND), :] + center) + (0.5 * TIME_STEP) * rate
            else:
                value = center + TIME_STEP * rate
            out[u, x, pl.ds(y, BAND), :] = value
        return carry

    lax.fori_loop(0, CY // BAND, band, 0)

    @pl.when(x == CX - 1)
    def _():
        scale = PENALTY * TIME_STEP * (0.5 if second else 1.0)

        def patch(s, carry):
            t = rows[0, s]
            a, b = t // CY, t % CY
            for v in range(NVAR):
                out[v, a, pl.ds(b, 1), :] -= scale * ext[v, a + 1, pl.ds(b + 8, 1), :]
            return carry

        lax.fori_loop(0, SLOTS, patch, 0)


TABLES = [
    pltpu.SMEM((CAP, PEERS), jnp.int32),
    pltpu.SMEM((1, PEERS), jnp.int32),
    pltpu.SMEM((CAP, PEERS), F32),
]
FIELD_V = pltpu.VMEM((NVAR, ROWS + 2 * EDGE, CZ), F32)
DATA_V = pltpu.VMEM((OTHERS * BLOCKS, PACK, CZ), F32)
ARRIVE = [
    pltpu.SMEM((6, NVAR * NVAR), F32),
    pltpu.SMEM((1, SLOTS), jnp.int32),
    pltpu.VMEM((COMPS, BLOCKS * CAP), jnp.int32),
    DATA_V,
    pltpu.VMEM((NVAR, SLOTS, CZ), F32),
    FIELD_V,
    pltpu.VMEM((NVAR, CY, CZ), F32),
    pltpu.VMEM((NVAR, CY, CZ), F32),
    pltpu.VMEM((2, CY, CZ), F32),
    DMA((12,)),
]


def call(kernel, name, inputs, out_shape, scratch, moved, flops):
    single = not isinstance(out_shape, list)
    return pl.pallas_call(
        kernel,
        in_specs=[HBM] * len(inputs),
        out_specs=HBM if single else [HBM] * len(out_shape),
        out_shape=out_shape,
        scratch_shapes=scratch,
        compiler_params=pltpu.CompilerParams(vmem_limit_bytes=VMEM_LIMIT),
        cost_estimate=pl.CostEstimate(flops=flops, bytes_accessed=moved, transcendentals=0),
        name=name,
    )(*inputs)


def pack(tables, field):
    return call(
        pack_kernel, "pack", [*tables, field], shape(PEERS, PACK, CZ),
        [*TABLES, FIELD_V, DATA_V, DMA((4,)), DMA((OTHERS,))], 8 << 20, 10**6,
    )


def middle(tables, inputs):
    plane = shape(NVAR, CY, CZ)
    return call(
        middle_kernel, "middle", [*tables, *inputs],
        [shape(PEERS, PACK, CZ), shape(NVAR, ROWS, CZ), plane, plane],
        [*TABLES, *ARRIVE, DMA((3,)), DMA((OTHERS,))], 16 << 20, 10**8,
    )


def finish(inputs):
    return call(finish_kernel, "finish", inputs, shape(NVAR, ROWS, CZ), ARRIVE, 10 << 20, 10**8)


def advance(second, coupling, rows, field, streams, volume):
    return pl.pallas_call(
        functools.partial(flux_kernel, second),
        grid=(CX,),
        in_specs=[SMEM, SMEM, HBM]
        + [pl.BlockSpec((NVAR, 1, CY, CZ), lambda i: (0, i, 0, 0))] * len(streams)
        + [pl.BlockSpec((1, CY, CZ), lambda i: (i, 0, 0))],
        out_specs=pl.BlockSpec((NVAR, CX, CY, CZ), lambda i: (0, 0, 0, 0)),
        out_shape=shape(NVAR, CX, CY, CZ),
        scratch_shapes=[pltpu.VMEM((NVAR, CX + 2, CY + 16, CZ), F32), DMA(())],
        compiler_params=pltpu.CompilerParams(dimension_semantics=("arbitrary",), vmem_limit_bytes=VMEM_LIMIT),
        cost_estimate=pl.CostEstimate(flops=60 * 10**6, bytes_accessed=40 << 20, transcendentals=0),
        name="advance_end" if second else "advance_mid",
    )(coupling, rows, field, *streams, volume)


def exchange(sent):
    return lax.all_to_all(sent, ("comp", "blk"), split_axis=0, concat_axis=0, tiled=True)


def halos(low, high):
    count = lax.axis_size("blk")
    below = lax.ppermute(high, "blk", [(i, i + 1) for i in range(count - 1)])
    above = lax.ppermute(low, "blk", [(i + 1, i) for i in range(count - 1)])
    return below, above


def shards(psi_start, adj_source, vol_inverse, coupling, send_tile, send_count, send_weight, recv_slot, fringe_row):
    start = psi_start[0]
    source = adj_source[0]
    volume = vol_inverse[0]
    matrices = coupling[0].reshape(6, NVAR * NVAR)
    tables = [send_tile[0].T, send_count, send_weight[0].T]
    slots = recv_slot[0].reshape(COMPS, BLOCKS * CAP)

    tiled = (NVAR, ROWS, CZ)

    arrived = exchange(pack(tables, start.reshape(tiled)))
    below, above = halos(start[:, 0], start[:, -1])
    mid = advance(False, matrices, fringe_row, start, [source], volume).reshape(tiled)
    sent, mid, low, high = middle(tables, [matrices, fringe_row, slots, arrived, mid, below, above, volume])
    arrived = exchange(sent)
    below, above = halos(low, high)
    end = advance(True, matrices, fringe_row, mid.reshape(NVAR, CX, CY, CZ), [start, source], volume)
    end = finish([matrices, fringe_row, slots, arrived, end.reshape(tiled), below, above, volume])
    return end.reshape(1, NVAR, CX, CY, CZ)


def solution(mesh):
    in_specs = (
        P("comp", None, "blk", None, None),
        P("comp", None, "blk", None, None),
        P("comp", "blk", None, None),
        P("comp", None, None, None),
        P(("comp", "blk"), None, None),
        P(("comp", "blk"), None),
        P(("comp", "blk"), None, None),
        P(("comp", "blk"), None, None),
        P(("comp", "blk"), None),
    )
    out_specs = P("comp", None, "blk", None, None)
    return jax.shard_map(shards, mesh=mesh, in_specs=in_specs, out_specs=out_specs, check_vma=False)
```

```python
import functools

import jax
import jax.numpy as jnp
from jax import lax
from jax.experimental import pallas as pl
from jax.experimental.pallas import tpu as pltpu
from jax.sharding import PartitionSpec as P

PENALTY = 4.0
TIME_STEP = 0.08
NVAR, CX, CY, CZ = 6, 8, 128, 128
ROWS = CX * CY
CAP = 8
SLOTS = 64
COMPS = 4
BLOCKS = 32
PEERS = COMPS * BLOCKS
OTHERS = COMPS - 1
PACK = NVAR * CAP
SPLIT = 2
PIECES = OTHERS * SPLIT
BAND = 32
EDGE = 8
BATCH = 4
WHOLE_VMEM = 67_000_000
VMEM_LIMIT = 63_500_000
F32 = jnp.float32
HBM = pl.BlockSpec(memory_space=pltpu.HBM)
SMEM = pl.BlockSpec(memory_space=pltpu.SMEM)
VMEM = pl.BlockSpec(memory_space=pltpu.VMEM)
DMA = pltpu.SemaphoreType.DMA


def shape(*dims):
    return jax.ShapeDtypeStruct(dims, F32)


def start_all(copies):
    for copy in copies:
        copy.start()


def wait_all(copies):
    for copy in copies:
        copy.wait()


def other(j):
    return lax.rem(lax.axis_index("comp") + j + 1, COMPS)


def block_of(ref, j):
    return ref.at[pl.ds(other(j) * BLOCKS, BLOCKS)]


def part_of(ref, j):
    return ref.at[pl.ds(j * BLOCKS, BLOCKS)]


def gather_rows(field, tables, buf, sent, sems):
    tile, count, weight = tables
    row_ids = lax.broadcasted_iota(jnp.int32, (CAP, CZ), 0)
    size = BLOCKS // SPLIT
    stores = []
    for piece in range(PIECES):
        first = other(piece // SPLIT) * BLOCKS + (piece % SPLIT) * size

        def peer_rows(b, carry):
            peer = first + b
            live = count[0, peer]
            spots = [tile[e, peer] + (EDGE - e) for e in range(CAP)]
            scale = jnp.full((CAP, CZ), weight[0, peer])
            for e in range(1, CAP):
                scale = jnp.where(row_ids == e, weight[e, peer], scale)
            scale = jnp.where(row_ids < live, scale, 0.0)
            for v in range(NVAR):
                rows = field[v, pl.ds(spots[0], CAP), :]
                for e in range(1, CAP):
                    rows = jnp.where(row_ids == e, field[v, pl.ds(spots[e], CAP), :], rows)
                buf[piece * size + b, v * CAP : (v + 1) * CAP, :] = rows * scale
            return carry

        lax.fori_loop(0, size, peer_rows, 0, unroll=4)
        ready = buf.at[pl.ds(piece * size, size)]
        stores.append(pltpu.make_async_copy(ready, sent.at[pl.ds(first, size)], sems.at[piece]))
        stores[-1].start()
    return stores


def reduce_rows(slots, loads, data, total):
    slot_ids = lax.broadcasted_iota(jnp.int32, (SLOTS, BLOCKS * CAP), 0)
    for j in range(OTHERS):
        onehot = (slots[pl.ds(other(j), 1), :] == slot_ids).astype(F32).astype(jnp.bfloat16)
        loads[j].wait()
        for v in range(NVAR):
            part = data[j * BLOCKS : (j + 1) * BLOCKS, v * CAP : (v + 1) * CAP, :].reshape(BLOCKS * CAP, CZ)
            high = part.astype(jnp.bfloat16)
            low = (part - high.astype(F32)).astype(jnp.bfloat16)
            both = jnp.dot(onehot, jnp.concatenate([high, low], axis=1), preferred_element_type=F32)
            both = both[:, :CZ] + both[:, CZ:]
            total[v] = both if j == 0 else total[v] + both


def settle(field, coupling, rows, total, below, above, volume, scale):
    for side, halo, first in ((1, below, EDGE), (0, above, EDGE + ROWS - CY)):

        def band(i, carry):
            y = pl.multiple_of(i * BAND, BAND)
            vol = volume[1 - side, pl.ds(y, BAND), :] * scale
            near = [halo[w, pl.ds(y, BAND), :] for w in range(NVAR)]
            for u in range(NVAR):
                flux = coupling[side, u] * near[0]
                for w in range(1, NVAR):
                    flux = flux + coupling[side, w * NVAR + u] * near[w]
                field[u, pl.ds(first + y, BAND), :] += vol * flux
            return carry

        lax.fori_loop(0, CY // BAND, band, 0)

    def patch(i, carry):
        slots = [i * BATCH + k for k in range(BATCH)]
        spots = [rows[0, s] + EDGE for s in slots]
        sums = []
        for s, t in zip(slots, spots):
            for v in range(NVAR):
                sums.append(field[v, pl.ds(t, 1), :] + (PENALTY * scale) * total[v, pl.ds(s, 1), :])
        for k, t in enumerate(spots):
            for v in range(NVAR):
                field[v, pl.ds(t, 1), :] = sums[k * NVAR + v]
        return carry

    lax.fori_loop(0, SLOTS // BATCH, patch, 0)


def inner(field, first=0, size=ROWS):
    return field.at[:, pl.ds(EDGE + first, size), :]


def copies_of(pairs, sems, first=0):
    return [pltpu.make_async_copy(a, b, sems.at[first + i]) for i, (a, b) in enumerate(pairs)]


def pack_kernel(tile, count, weight, field, sent, tile_s, count_s, weight_s, field_v, buf, sems, sent_sems):
    scratch = (tile_s, count_s, weight_s)
    copies = copies_of(list(zip((tile, count, weight), scratch)) + [(field, inner(field_v))], sems)
    start_all(copies)
    wait_all(copies)
    wait_all(gather_rows(field_v, scratch, buf, sent, sent_sems))


def arrive(inputs, scratch, sems, field, scale):
    coupling, rows, slots, arrived, below, above, volume = inputs
    coupling_s, rows_s, slots_v, data, total, below_v, above_v, volume_v = scratch
    loads = [(slots, slots_v)] + [(block_of(arrived, j), part_of(data, j)) for j in range(OTHERS)]
    others = [(coupling, coupling_s), (rows, rows_s), (below, below_v), (above, above_v)]
    others += [(volume.at[0], volume_v.at[0]), (volume.at[CX - 1], volume_v.at[1])]
    loads = copies_of(loads, sems)
    others = copies_of(others, sems, len(loads))
    start_all(loads + others)
    loads[0].wait()
    reduce_rows(slots_v, loads[1:], data, total)
    wait_all(others)
    settle(field, coupling_s, rows_s, total, below_v, above_v, volume_v, scale)


def middle_kernel(*refs):
    tables, inputs, refs = refs[:3], refs[4:11], refs[11:]
    field, sent, mid, low, high, refs = *refs[:5], refs[5:]
    table_scratch, scratch, (sems, table_sems, sent_sems) = refs[:3], refs[3:11], refs[11:]
    table_copies = copies_of(list(zip(tables, table_scratch)), table_sems)
    start_all(table_copies)
    arrive(inputs, scratch, sems, field, TIME_STEP)
    stores = copies_of([(inner(field), mid), (inner(field, 0, CY), low), (inner(field, ROWS - CY, CY), high)], sems)
    start_all(stores)
    wait_all(table_copies)
    wait_all(gather_rows(field, table_scratch, scratch[3], sent, sent_sems))
    wait_all(stores)


def finish_kernel(*refs):
    inputs, (field, end), scratch, sems = refs[1:8], refs[8:10], refs[10:18], refs[18]
    arrive(inputs, scratch, sems, field, 0.5 * TIME_STEP)
    store = pltpu.make_async_copy(inner(field), end, sems.at[0])
    store.start()
    store.wait()


def flux_kernel(second, coupling, rows, field, *refs):
    if second:
        base, source, volume, out, ext, sem = refs
    else:
        source, volume, out, ext, sem = refs
    x = pl.program_id(0)

    @pl.when(x == 0)
    def _():
        copy = pltpu.make_async_copy(field, ext.at[:, pl.ds(1, CX), pl.ds(8, CY), :], sem)
        copy.start()
        edge = jnp.zeros((NVAR, CX + 2, 8, CZ), F32)
        ext[:, :, 0:8, :] = edge
        ext[:, :, 8 + CY : 16 + CY, :] = edge
        plane = jnp.zeros((NVAR, CY, CZ), F32)
        ext[:, 0, 8 : 8 + CY, :] = plane
        ext[:, CX + 1, 8 : 8 + CY, :] = plane
        copy.wait()

    lane = lax.broadcasted_iota(jnp.int32, (BAND, CZ), 1)

    def band(i, carry):
        y = pl.multiple_of(i * BAND, BAND)
        flux = [jnp.zeros((BAND, CZ), F32) for _ in range(NVAR)]
        for w in range(NVAR):
            center = ext[w, x + 1, pl.ds(y + 8, BAND), :]
            for d in range(6):
                if d == 0:
                    near = ext[w, x + 2, pl.ds(y + 8, BAND), :]
                elif d == 1:
                    near = ext[w, x, pl.ds(y + 8, BAND), :]
                elif d == 2:
                    near = ext[w, x + 1, pl.ds(y + 9, BAND), :]
                elif d == 3:
                    near = ext[w, x + 1, pl.ds(y + 7, BAND), :]
                elif d == 4:
                    near = jnp.where(lane == CZ - 1, 0.0, pltpu.roll(center, CZ - 1, 1))
                else:
                    near = jnp.where(lane == 0, 0.0, pltpu.roll(center, 1, 1))
                diff = near - center
                for u in range(NVAR):
                    flux[u] = flux[u] + coupling[d, w * NVAR + u] * diff
        vol = volume[0, pl.ds(y, BAND), :]
        for u in range(NVAR):
            rate = vol * flux[u] + source[u, 0, pl.ds(y, BAND), :]
            center = ext[u, x + 1, pl.ds(y + 8, BAND), :]
            if second:
                value = 0.5 * (base[u, 0, pl.ds(y, BAND), :] + center) + (0.5 * TIME_STEP) * rate
            else:
                value = center + TIME_STEP * rate
            out[u, pl.ds(EDGE + x * CY + y, BAND), :] = value
        return carry

    lax.fori_loop(0, CY // BAND, band, 0)

    @pl.when(x == CX - 1)
    def _():
        scale = PENALTY * TIME_STEP * (0.5 if second else 1.0)

        def patch(s, carry):
            t = rows[0, s]
            a, b = t // CY, t % CY
            for v in range(NVAR):
                out[v, pl.ds(t + EDGE, 1), :] -= scale * ext[v, a + 1, pl.ds(b + 8, 1), :]
            return carry

        lax.fori_loop(0, SLOTS, patch, 0)


TABLES = [
    pltpu.SMEM((CAP, PEERS), jnp.int32),
    pltpu.SMEM((1, PEERS), jnp.int32),
    pltpu.SMEM((CAP, PEERS), F32),
]
FIELD_V = pltpu.VMEM((NVAR, ROWS + 2 * EDGE, CZ), F32)
DATA_V = pltpu.VMEM((OTHERS * BLOCKS, PACK, CZ), F32)
ARRIVE = [
    pltpu.SMEM((6, NVAR * NVAR), F32),
    pltpu.SMEM((1, SLOTS), jnp.int32),
    pltpu.VMEM((COMPS, BLOCKS * CAP), jnp.int32),
    DATA_V,
    pltpu.VMEM((NVAR, SLOTS, CZ), F32),
    pltpu.VMEM((NVAR, CY, CZ), F32),
    pltpu.VMEM((NVAR, CY, CZ), F32),
    pltpu.VMEM((2, CY, CZ), F32),
    DMA((10,)),
]


def call(kernel, name, inputs, out_shape, scratch, moved, flops, limit, held=None):
    specs = [HBM] * len(inputs)
    out_specs = [HBM] * len(out_shape)
    aliases = {}
    if held is not None:
        specs[held] = out_specs[0] = VMEM
        aliases = {held: 0}
    return pl.pallas_call(
        kernel,
        in_specs=specs,
        out_specs=out_specs,
        out_shape=out_shape,
        scratch_shapes=scratch,
        input_output_aliases=aliases,
        compiler_params=pltpu.CompilerParams(vmem_limit_bytes=limit),
        cost_estimate=pl.CostEstimate(flops=flops, bytes_accessed=moved, transcendentals=0),
        name=name,
    )(*inputs)


def pack(tables, field):
    (sent,) = call(
        pack_kernel, "pack", [*tables, field], [shape(PEERS, PACK, CZ)],
        [*TABLES, FIELD_V, DATA_V, DMA((4,)), DMA((PIECES,))], 8 << 20, 10**6, WHOLE_VMEM,
    )
    return sent


def middle(tables, field, inputs):
    return call(
        middle_kernel, "middle", [*tables, field, *inputs],
        [FIELD_V, shape(PEERS, PACK, CZ), shape(NVAR, ROWS, CZ), shape(NVAR, CY, CZ), shape(NVAR, CY, CZ)],
        [*TABLES, *ARRIVE, DMA((3,)), DMA((PIECES,))], 16 << 20, 10**8, VMEM_LIMIT, 3,
    )[1:]


def finish(field, inputs):
    out_shape = [FIELD_V, shape(NVAR, ROWS, CZ)]
    return call(finish_kernel, "finish", [field, *inputs], out_shape, ARRIVE, 10 << 20, 10**8, VMEM_LIMIT, 0)[1]


def advance(second, coupling, rows, field, streams, volume):
    return pl.pallas_call(
        functools.partial(flux_kernel, second),
        grid=(CX,),
        in_specs=[SMEM, SMEM, HBM]
        + [pl.BlockSpec((NVAR, 1, CY, CZ), lambda i: (0, i, 0, 0))] * len(streams)
        + [pl.BlockSpec((1, CY, CZ), lambda i: (i, 0, 0))],
        out_specs=VMEM,
        out_shape=FIELD_V,
        scratch_shapes=[pltpu.VMEM((NVAR, CX + 2, CY + 16, CZ), F32), DMA(())],
        compiler_params=pltpu.CompilerParams(dimension_semantics=("arbitrary",), vmem_limit_bytes=VMEM_LIMIT),
        cost_estimate=pl.CostEstimate(flops=60 * 10**6, bytes_accessed=40 << 20, transcendentals=0),
        name="advance_end" if second else "advance_mid",
    )(coupling, rows, field, *streams, volume)


def exchange(sent):
    return lax.all_to_all(sent, ("comp", "blk"), split_axis=0, concat_axis=0, tiled=True)


def halos(low, high):
    count = lax.axis_size("blk")
    below = lax.ppermute(high, "blk", [(i, i + 1) for i in range(count - 1)])
    above = lax.ppermute(low, "blk", [(i + 1, i) for i in range(count - 1)])
    return below, above


def shards(psi_start, adj_source, vol_inverse, coupling, send_tile, send_count, send_weight, recv_slot, fringe_row):
    start = psi_start[0]
    source = adj_source[0]
    volume = vol_inverse[0]
    matrices = coupling[0].reshape(6, NVAR * NVAR)
    tables = [send_tile[0].T, send_count, send_weight[0].T]
    slots = recv_slot[0].reshape(COMPS, BLOCKS * CAP)

    tiled = (NVAR, ROWS, CZ)

    arrived = exchange(pack(tables, start.reshape(tiled)))
    below, above = halos(start[:, 0], start[:, -1])
    field = advance(False, matrices, fringe_row, start, [source], volume)
    sent, mid, low, high = middle(tables, field, [matrices, fringe_row, slots, arrived, below, above, volume])
    arrived = exchange(sent)
    below, above = halos(low, high)
    field = advance(True, matrices, fringe_row, mid.reshape(NVAR, CX, CY, CZ), [start, source], volume)
    end = finish(field, [matrices, fringe_row, slots, arrived, below, above, volume])
    return end.reshape(1, NVAR, CX, CY, CZ)


def solution(mesh):
    in_specs = (
        P("comp", None, "blk", None, None),
        P("comp", None, "blk", None, None),
        P("comp", "blk", None, None),
        P("comp", None, None, None),
        P(("comp", "blk"), None, None),
        P(("comp", "blk"), None),
        P(("comp", "blk"), None, None),
        P(("comp", "blk"), None, None),
        P(("comp", "blk"), None),
    )
    out_specs = P("comp", None, "blk", None, None)
    return jax.shard_map(shards, mesh=mesh, in_specs=in_specs, out_specs=out_specs, check_vma=False)
```

```python
import functools

import jax
import jax.numpy as jnp
from jax import lax
from jax.experimental import pallas as pl
from jax.experimental.pallas import tpu as pltpu
from jax.sharding import PartitionSpec as P

PENALTY = 4.0
TIME_STEP = 0.08
NVAR, CX, CY, CZ = 6, 8, 128, 128
ROWS = CX * CY
CAP = 8
SLOTS = 64
COMPS = 4
BLOCKS = 32
PEERS = COMPS * BLOCKS
OTHERS = COMPS - 1
PACK = NVAR * CAP
SPLIT = 4
PIECES = OTHERS * SPLIT
BAND = 32
EDGE = 8
BATCH = 4
HALF = 3
WHOLE_VMEM = 67_000_000
VMEM_LIMIT = 63_500_000
F32 = jnp.float32
HBM = pl.BlockSpec(memory_space=pltpu.HBM)
SMEM = pl.BlockSpec(memory_space=pltpu.SMEM)
VMEM = pl.BlockSpec(memory_space=pltpu.VMEM)
DMA = pltpu.SemaphoreType.DMA


def shape(*dims):
    return jax.ShapeDtypeStruct(dims, F32)


def start_all(copies):
    for copy in copies:
        copy.start()


def wait_all(copies):
    for copy in copies:
        copy.wait()


def other(j):
    return lax.rem(lax.axis_index("comp") + j + 1, COMPS)


def block_of(ref, j):
    return ref.at[pl.ds(other(j) * BLOCKS, BLOCKS)]


def part_of(ref, j):
    return ref.at[pl.ds(j * BLOCKS, BLOCKS)]


def gather_rows(field, tables, buf, sent, sems):
    tile, count, weight = tables
    row_ids = lax.broadcasted_iota(jnp.int32, (CAP, CZ), 0)
    size = BLOCKS // SPLIT
    stores = []
    for piece in range(PIECES):
        first = other(piece // SPLIT) * BLOCKS + (piece % SPLIT) * size

        def peer_rows(b, carry):
            peer = first + b
            live = count[0, peer]
            spots = [tile[e, peer] + (EDGE - e) for e in range(CAP)]
            scale = jnp.full((CAP, CZ), weight[0, peer])
            for e in range(1, CAP):
                scale = jnp.where(row_ids == e, weight[e, peer], scale)
            scale = jnp.where(row_ids < live, scale, 0.0)
            for v in range(NVAR):
                rows = field[v, pl.ds(spots[0], CAP), :]
                for e in range(1, CAP):
                    rows = jnp.where(row_ids == e, field[v, pl.ds(spots[e], CAP), :], rows)
                buf[piece * size + b, v * CAP : (v + 1) * CAP, :] = rows * scale
            return carry

        lax.fori_loop(0, size, peer_rows, 0, unroll=4)
        ready = buf.at[pl.ds(piece * size, size)]
        stores.append(pltpu.make_async_copy(ready, sent.at[pl.ds(first, size)], sems.at[piece]))
        stores[-1].start()
    return stores


def reduce_rows(slots, loads, data, total):
    slot_ids = lax.broadcasted_iota(jnp.int32, (SLOTS, BLOCKS * CAP), 0)
    for j in range(OTHERS):
        onehot = (slots[pl.ds(other(j), 1), :] == slot_ids).astype(F32).astype(jnp.bfloat16)
        loads[j].wait()
        for v in range(NVAR):
            part = data[j * BLOCKS : (j + 1) * BLOCKS, v * CAP : (v + 1) * CAP, :].reshape(BLOCKS * CAP, CZ)
            high = part.astype(jnp.bfloat16)
            low = (part - high.astype(F32)).astype(jnp.bfloat16)
            both = jnp.dot(onehot, jnp.concatenate([high, low], axis=1), preferred_element_type=F32)
            both = both[:, :CZ] + both[:, CZ:]
            total[v] = both if j == 0 else total[v] + both


def add_halos(field, coupling, below, above, volume, scale):
    for side, halo, first in ((1, below, EDGE), (0, above, EDGE + ROWS - CY)):

        def band(i, carry):
            y = pl.multiple_of(i * BAND, BAND)
            vol = volume[1 - side, pl.ds(y, BAND), :] * scale
            near = [halo[w, pl.ds(y, BAND), :] for w in range(NVAR)]
            for u in range(NVAR):
                flux = coupling[side, u] * near[0]
                for w in range(1, NVAR):
                    flux = flux + coupling[side, w * NVAR + u] * near[w]
                field[u, pl.ds(first + y, BAND), :] += vol * flux
            return carry

        lax.fori_loop(0, CY // BAND, band, 0)


def patch_rows(field, rows, total, scale, variables):
    def patch(i, carry):
        slots = [i * BATCH + k for k in range(BATCH)]
        spots = [rows[0, s] + EDGE for s in slots]
        sums = []
        for s, t in zip(slots, spots):
            for v in variables:
                sums.append(field[v, pl.ds(t, 1), :] + (PENALTY * scale) * total[v, pl.ds(s, 1), :])
        for k, t in enumerate(spots):
            for n, v in enumerate(variables):
                field[v, pl.ds(t, 1), :] = sums[k * len(variables) + n]
        return carry

    lax.fori_loop(0, SLOTS // BATCH, patch, 0)


def inner(field, first=0, size=ROWS):
    return field.at[:, pl.ds(EDGE + first, size), :]


def line(field, v):
    return field.at[v, pl.ds(EDGE, ROWS), :]


def copies_of(pairs, sems, first=0):
    return [pltpu.make_async_copy(a, b, sems.at[first + i]) for i, (a, b) in enumerate(pairs)]


def pack_kernel(tile, count, weight, field, sent, tile_s, count_s, weight_s, field_v, buf, sems, sent_sems):
    scratch = (tile_s, count_s, weight_s)
    pairs = list(zip((tile, count, weight), scratch)) + [(field.at[v], line(field_v, v)) for v in range(NVAR)]
    copies = copies_of(pairs, sems)
    start_all(copies)
    wait_all(copies)
    wait_all(gather_rows(field_v, scratch, buf, sent, sent_sems))


def arrive(inputs, scratch, sems, field, scale):
    coupling, rows, slots, arrived, below, above, volume = inputs
    coupling_s, rows_s, slots_v, data, total, below_v, above_v, volume_v = scratch
    first = [(coupling, coupling_s), (below, below_v), (above, above_v)]
    first += [(volume.at[0], volume_v.at[0]), (volume.at[CX - 1], volume_v.at[1])]
    first += [(slots, slots_v), (rows, rows_s)]
    loads = [(block_of(arrived, j), part_of(data, j)) for j in range(OTHERS)]
    first = copies_of(first, sems)
    loads = copies_of(loads, sems, len(first))
    start_all(first + loads)
    wait_all(first)
    add_halos(field, coupling_s, below_v, above_v, volume_v, scale)
    reduce_rows(slots_v, loads, data, total)


def middle_kernel(*refs):
    tables, inputs, refs = refs[:3], refs[4:11], refs[11:]
    field, sent, low, high, refs = *refs[:4], refs[4:]
    table_scratch, scratch, (sems, table_sems, sent_sems) = refs[:3], refs[3:11], refs[11:]
    table_copies = copies_of(list(zip(tables, table_scratch)), table_sems)
    start_all(table_copies)
    arrive(inputs, scratch, sems, field, TIME_STEP)
    patch_rows(field, scratch[1], scratch[4], TIME_STEP, range(NVAR))
    stores = copies_of([(inner(field, 0, CY), low), (inner(field, ROWS - CY, CY), high)], sems)
    start_all(stores)
    wait_all(table_copies)
    wait_all(gather_rows(field, table_scratch, scratch[3], sent, sent_sems))
    wait_all(stores)


def spill_kernel(field, held, mid, sem):
    store = pltpu.make_async_copy(inner(held), mid, sem)
    store.start()
    store.wait()


def finish_kernel(*refs):
    inputs, (field, end), scratch, sems = refs[1:8], refs[8:10], refs[10:18], refs[18]
    arrive(inputs, scratch, sems, field, 0.5 * TIME_STEP)
    stores = copies_of([(line(field, v), end.at[v]) for v in range(NVAR)], sems)
    for first in range(0, NVAR, HALF):
        half = range(first, first + HALF)
        patch_rows(field, scratch[1], scratch[4], 0.5 * TIME_STEP, half)
        start_all([stores[v] for v in half])
    wait_all(stores)


def flux_kernel(second, coupling, rows, field, *refs):
    if second:
        base, source, volume, out, ext, sems = refs
    else:
        source, volume, out, ext, sems = refs
    x = pl.program_id(0)

    @pl.when(x == 0)
    def _():
        planes = [(field.at[:, i], ext.at[:, i + 1, pl.ds(8, CY), :]) for i in range(CX)]
        copies = copies_of(planes, sems)
        start_all(copies)
        edge = jnp.zeros((NVAR, CX + 2, 8, CZ), F32)
        ext[:, :, 0:8, :] = edge
        ext[:, :, 8 + CY : 16 + CY, :] = edge
        plane = jnp.zeros((NVAR, CY, CZ), F32)
        ext[:, 0, 8 : 8 + CY, :] = plane
        ext[:, CX + 1, 8 : 8 + CY, :] = plane
        wait_all(copies)

    lane = lax.broadcasted_iota(jnp.int32, (BAND, CZ), 1)

    def band(i, carry):
        y = pl.multiple_of(i * BAND, BAND)
        flux = [jnp.zeros((BAND, CZ), F32) for _ in range(NVAR)]
        for w in range(NVAR):
            center = ext[w, x + 1, pl.ds(y + 8, BAND), :]
            for d in range(6):
                if d == 0:
                    near = ext[w, x + 2, pl.ds(y + 8, BAND), :]
                elif d == 1:
                    near = ext[w, x, pl.ds(y + 8, BAND), :]
                elif d == 2:
                    near = ext[w, x + 1, pl.ds(y + 9, BAND), :]
                elif d == 3:
                    near = ext[w, x + 1, pl.ds(y + 7, BAND), :]
                elif d == 4:
                    near = jnp.where(lane == CZ - 1, 0.0, pltpu.roll(center, CZ - 1, 1))
                else:
                    near = jnp.where(lane == 0, 0.0, pltpu.roll(center, 1, 1))
                diff = near - center
                for u in range(NVAR):
                    flux[u] = flux[u] + coupling[d, w * NVAR + u] * diff
        vol = volume[0, pl.ds(y, BAND), :]
        for u in range(NVAR):
            rate = vol * flux[u] + source[u, 0, pl.ds(y, BAND), :]
            center = ext[u, x + 1, pl.ds(y + 8, BAND), :]
            if second:
                value = 0.5 * (base[u, 0, pl.ds(y, BAND), :] + center) + (0.5 * TIME_STEP) * rate
            else:
                value = center + TIME_STEP * rate
            out[u, pl.ds(EDGE + x * CY + y, BAND), :] = value
        return carry

    lax.fori_loop(0, CY // BAND, band, 0)

    @pl.when(x == CX - 1)
    def _():
        scale = PENALTY * TIME_STEP * (0.5 if second else 1.0)

        def patch(s, carry):
            t = rows[0, s]
            a, b = t // CY, t % CY
            for v in range(NVAR):
                out[v, pl.ds(t + EDGE, 1), :] -= scale * ext[v, a + 1, pl.ds(b + 8, 1), :]
            return carry

        lax.fori_loop(0, SLOTS, patch, 0)


TABLES = [
    pltpu.SMEM((CAP, PEERS), jnp.int32),
    pltpu.SMEM((1, PEERS), jnp.int32),
    pltpu.SMEM((CAP, PEERS), F32),
]
FIELD_V = pltpu.VMEM((NVAR, ROWS + 2 * EDGE, CZ), F32)
DATA_V = pltpu.VMEM((OTHERS * BLOCKS, PACK, CZ), F32)
ARRIVE = [
    pltpu.SMEM((6, NVAR * NVAR), F32),
    pltpu.SMEM((1, SLOTS), jnp.int32),
    pltpu.VMEM((COMPS, BLOCKS * CAP), jnp.int32),
    DATA_V,
    pltpu.VMEM((NVAR, SLOTS, CZ), F32),
    pltpu.VMEM((NVAR, CY, CZ), F32),
    pltpu.VMEM((NVAR, CY, CZ), F32),
    pltpu.VMEM((2, CY, CZ), F32),
    DMA((10,)),
]


def call(kernel, name, inputs, out_shape, scratch, moved, flops, limit, held=None):
    specs = [HBM] * len(inputs)
    out_specs = [HBM] * len(out_shape)
    aliases = {}
    if held is not None:
        specs[held] = out_specs[0] = VMEM
        aliases = {held: 0}
    return pl.pallas_call(
        kernel,
        in_specs=specs,
        out_specs=out_specs,
        out_shape=out_shape,
        scratch_shapes=scratch,
        input_output_aliases=aliases,
        compiler_params=pltpu.CompilerParams(vmem_limit_bytes=limit),
        cost_estimate=pl.CostEstimate(flops=flops, bytes_accessed=moved, transcendentals=0),
        name=name,
    )(*inputs)


def pack(tables, field):
    (sent,) = call(
        pack_kernel, "pack", [*tables, field], [shape(PEERS, PACK, CZ)],
        [*TABLES, FIELD_V, DATA_V, DMA((3 + NVAR,)), DMA((PIECES,))], 8 << 20, 10**6, WHOLE_VMEM,
    )
    return sent


def middle(tables, field, inputs):
    return call(
        middle_kernel, "middle", [*tables, field, *inputs],
        [FIELD_V, shape(PEERS, PACK, CZ), shape(NVAR, CY, CZ), shape(NVAR, CY, CZ)],
        [*TABLES, *ARRIVE, DMA((3,)), DMA((PIECES,))], 16 << 20, 10**8, VMEM_LIMIT, 3,
    )


def spill(field):
    out_shape = [FIELD_V, shape(NVAR, ROWS, CZ)]
    return call(spill_kernel, "spill", [field], out_shape, [DMA(())], 3 << 20, 10**6, VMEM_LIMIT, 0)[1]


def finish(field, inputs):
    out_shape = [FIELD_V, shape(NVAR, ROWS, CZ)]
    return call(finish_kernel, "finish", [field, *inputs], out_shape, ARRIVE, 10 << 20, 10**8, VMEM_LIMIT, 0)[1]


def advance(second, coupling, rows, field, streams, volume):
    return pl.pallas_call(
        functools.partial(flux_kernel, second),
        grid=(CX,),
        in_specs=[SMEM, SMEM, HBM]
        + [pl.BlockSpec((NVAR, 1, CY, CZ), lambda i: (0, i, 0, 0))] * len(streams)
        + [pl.BlockSpec((1, CY, CZ), lambda i: (i, 0, 0))],
        out_specs=VMEM,
        out_shape=FIELD_V,
        scratch_shapes=[pltpu.VMEM((NVAR, CX + 2, CY + 16, CZ), F32), DMA((CX,))],
        compiler_params=pltpu.CompilerParams(dimension_semantics=("arbitrary",), vmem_limit_bytes=VMEM_LIMIT),
        cost_estimate=pl.CostEstimate(flops=60 * 10**6, bytes_accessed=40 << 20, transcendentals=0),
        name="advance_end" if second else "advance_mid",
    )(coupling, rows, field, *streams, volume)


def exchange(sent):
    return lax.all_to_all(sent, ("comp", "blk"), split_axis=0, concat_axis=0, tiled=True)


def halos(low, high):
    count = lax.axis_size("blk")
    below = lax.ppermute(high, "blk", [(i, i + 1) for i in range(count - 1)])
    above = lax.ppermute(low, "blk", [(i + 1, i) for i in range(count - 1)])
    return below, above


def shards(psi_start, adj_source, vol_inverse, coupling, send_tile, send_count, send_weight, recv_slot, fringe_row):
    start = psi_start[0]
    source = adj_source[0]
    volume = vol_inverse[0]
    matrices = coupling[0].reshape(6, NVAR * NVAR)
    tables = [send_tile[0].T, send_count, send_weight[0].T]
    slots = recv_slot[0].reshape(COMPS, BLOCKS * CAP)

    tiled = (NVAR, ROWS, CZ)

    arrived = exchange(pack(tables, start.reshape(tiled)))
    below, above = halos(start[:, 0], start[:, -1])
    field = advance(False, matrices, fringe_row, start, [source], volume)
    field, sent, low, high = middle(tables, field, [matrices, fringe_row, slots, arrived, below, above, volume])
    arrived = exchange(sent)
    mid = spill(field)
    below, above = halos(low, high)
    field = advance(True, matrices, fringe_row, mid.reshape(NVAR, CX, CY, CZ), [start, source], volume)
    end = finish(field, [matrices, fringe_row, slots, arrived, below, above, volume])
    return end.reshape(1, NVAR, CX, CY, CZ)


def solution(mesh):
    in_specs = (
        P("comp", None, "blk", None, None),
        P("comp", None, "blk", None, None),
        P("comp", "blk", None, None),
        P("comp", None, None, None),
        P(("comp", "blk"), None, None),
        P(("comp", "blk"), None),
        P(("comp", "blk"), None, None),
        P(("comp", "blk"), None, None),
        P(("comp", "blk"), None),
    )
    out_specs = P("comp", None, "blk", None, None)
    return jax.shard_map(shards, mesh=mesh, in_specs=in_specs, out_specs=out_specs, check_vma=False)
```

```python
import functools

import jax
import jax.numpy as jnp
from jax import lax
from jax.experimental import pallas as pl
from jax.experimental.pallas import tpu as pltpu
from jax.sharding import PartitionSpec as P

PENALTY = 4.0
TIME_STEP = 0.08
NVAR, CX, CY, CZ = 6, 8, 128, 128
ROWS = CX * CY
CAP = 8
SLOTS = 64
COMPS = 4
BLOCKS = 32
PEERS = COMPS * BLOCKS
OTHERS = COMPS - 1
PACK = NVAR * CAP
SPLIT = 4
PIECES = OTHERS * SPLIT
BAND = 32
EDGE = 8
BATCH = 4
HALF = 3
LOADS = 4
WHOLE_VMEM = 67_000_000
VMEM_LIMIT = 63_500_000
F32 = jnp.float32
HBM = pl.BlockSpec(memory_space=pltpu.HBM)
SMEM = pl.BlockSpec(memory_space=pltpu.SMEM)
VMEM = pl.BlockSpec(memory_space=pltpu.VMEM)
DMA = pltpu.SemaphoreType.DMA


def shape(*dims):
    return jax.ShapeDtypeStruct(dims, F32)


def start_all(copies):
    for copy in copies:
        copy.start()


def wait_all(copies):
    for copy in copies:
        copy.wait()


def other(j):
    return lax.rem(lax.axis_index("comp") + j + 1, COMPS)


def block_of(ref, j):
    return ref.at[pl.ds(other(j) * BLOCKS, BLOCKS)]


def part_of(ref, j):
    return ref.at[pl.ds(j * BLOCKS, BLOCKS)]


def gather_rows(field, tables, buf, sent, sems):
    tile, count, weight = tables
    row_ids = lax.broadcasted_iota(jnp.int32, (CAP, CZ), 0)
    size = BLOCKS // SPLIT
    stores = []
    for piece in range(PIECES):
        first = other(piece // SPLIT) * BLOCKS + (piece % SPLIT) * size

        def peer_rows(b, carry):
            peer = first + b
            live = count[0, peer]
            spots = [tile[e, peer] + (EDGE - e) for e in range(CAP)]
            scale = jnp.full((CAP, CZ), weight[0, peer])
            for e in range(1, CAP):
                scale = jnp.where(row_ids == e, weight[e, peer], scale)
            scale = jnp.where(row_ids < live, scale, 0.0)
            for v in range(NVAR):
                rows = field[v, pl.ds(spots[0], CAP), :]
                for e in range(1, CAP):
                    rows = jnp.where(row_ids == e, field[v, pl.ds(spots[e], CAP), :], rows)
                buf[piece * size + b, v * CAP : (v + 1) * CAP, :] = rows * scale
            return carry

        lax.fori_loop(0, size, peer_rows, 0, unroll=4)
        ready = buf.at[pl.ds(piece * size, size)]
        stores.append(pltpu.make_async_copy(ready, sent.at[pl.ds(first, size)], sems.at[piece]))
        stores[-1].start()
    return stores


def reduce_rows(slots, loads, data, total):
    slot_ids = lax.broadcasted_iota(jnp.int32, (SLOTS, BLOCKS * CAP), 0)
    for j in range(OTHERS):
        onehot = (slots[pl.ds(other(j), 1), :] == slot_ids).astype(F32).astype(jnp.bfloat16)
        wait_all(loads[j * LOADS : (j + 1) * LOADS])
        for v in range(NVAR):
            part = data[j * BLOCKS : (j + 1) * BLOCKS, v * CAP : (v + 1) * CAP, :].reshape(BLOCKS * CAP, CZ)
            high = part.astype(jnp.bfloat16)
            low = (part - high.astype(F32)).astype(jnp.bfloat16)
            both = jnp.dot(onehot, jnp.concatenate([high, low], axis=1), preferred_element_type=F32)
            both = both[:, :CZ] + both[:, CZ:]
            total[v] = both if j == 0 else total[v] + both


def add_halos(field, coupling, below, above, volume, scale):
    for side, halo, first in ((1, below, EDGE), (0, above, EDGE + ROWS - CY)):

        def band(i, carry):
            y = pl.multiple_of(i * BAND, BAND)
            vol = volume[1 - side, pl.ds(y, BAND), :] * scale
            near = [halo[w, pl.ds(y, BAND), :] for w in range(NVAR)]
            for u in range(NVAR):
                flux = coupling[side, u] * near[0]
                for w in range(1, NVAR):
                    flux = flux + coupling[side, w * NVAR + u] * near[w]
                field[u, pl.ds(first + y, BAND), :] += vol * flux
            return carry

        lax.fori_loop(0, CY // BAND, band, 0)


def patch_rows(field, rows, total, scale, variables):
    def patch(i, carry):
        slots = [i * BATCH + k for k in range(BATCH)]
        spots = [rows[0, s] + EDGE for s in slots]
        sums = []
        for s, t in zip(slots, spots):
            for v in variables:
                sums.append(field[v, pl.ds(t, 1), :] + (PENALTY * scale) * total[v, pl.ds(s, 1), :])
        for k, t in enumerate(spots):
            for n, v in enumerate(variables):
                field[v, pl.ds(t, 1), :] = sums[k * len(variables) + n]
        return carry

    lax.fori_loop(0, SLOTS // BATCH, patch, 0)


def inner(field, first=0, size=ROWS):
    return field.at[:, pl.ds(EDGE + first, size), :]


def line(field, v):
    return field.at[v, pl.ds(EDGE, ROWS), :]


def copies_of(pairs, sems, first=0):
    return [pltpu.make_async_copy(a, b, sems.at[first + i]) for i, (a, b) in enumerate(pairs)]


def pack_kernel(tile, count, weight, field, sent, tile_s, count_s, weight_s, field_v, buf, sems, sent_sems):
    scratch = (tile_s, count_s, weight_s)
    pairs = list(zip((tile, count, weight), scratch)) + [(field.at[v], line(field_v, v)) for v in range(NVAR)]
    copies = copies_of(pairs, sems)
    start_all(copies)
    wait_all(copies)
    wait_all(gather_rows(field_v, scratch, buf, sent, sent_sems))


def arrive(inputs, scratch, sems, field, scale):
    coupling, rows, slots, arrived, below, above, volume = inputs
    coupling_s, rows_s, slots_v, data, total, below_v, above_v, volume_v = scratch
    first = [(coupling, coupling_s), (below, below_v), (above, above_v)]
    first += [(volume.at[0], volume_v.at[0]), (volume.at[CX - 1], volume_v.at[1])]
    first += [(slots, slots_v), (rows, rows_s)]
    size = BLOCKS // LOADS
    loads = []
    for j in range(OTHERS):
        for i in range(LOADS):
            span = pl.ds(i * size, size)
            loads.append((block_of(arrived, j).at[span], part_of(data, j).at[span]))
    first = copies_of(first, sems)
    loads = copies_of(loads, sems, len(first))
    start_all(first + loads)
    wait_all(first)
    add_halos(field, coupling_s, below_v, above_v, volume_v, scale)
    reduce_rows(slots_v, loads, data, total)


def middle_kernel(*refs):
    tables, inputs, refs = refs[:3], refs[4:11], refs[11:]
    field, sent, refs = *refs[:2], refs[2:]
    table_scratch, scratch, (sems, table_sems, sent_sems) = refs[:3], refs[3:11], refs[11:]
    table_copies = copies_of(list(zip(tables, table_scratch)), table_sems)
    start_all(table_copies)
    arrive(inputs, scratch, sems, field, TIME_STEP)
    patch_rows(field, scratch[1], scratch[4], TIME_STEP, range(NVAR))
    wait_all(table_copies)
    wait_all(gather_rows(field, table_scratch, scratch[3], sent, sent_sems))


def spill_kernel(field, held, mid, low, high, sems):
    pairs = [(inner(held, 0, CY), low), (inner(held, ROWS - CY, CY), high), (inner(held), mid)]
    stores = copies_of(pairs, sems)
    start_all(stores)
    wait_all(stores)


def finish_kernel(*refs):
    inputs, (field, end), scratch, sems = refs[1:8], refs[8:10], refs[10:18], refs[18]
    arrive(inputs, scratch, sems, field, 0.5 * TIME_STEP)
    stores = copies_of([(line(field, v), end.at[v]) for v in range(NVAR)], sems)
    for first in range(0, NVAR, HALF):
        half = range(first, first + HALF)
        patch_rows(field, scratch[1], scratch[4], 0.5 * TIME_STEP, half)
        start_all([stores[v] for v in half])
    wait_all(stores)


def flux_kernel(second, coupling, rows, field, *refs):
    if second:
        base, source, volume, out, ext, sems = refs
    else:
        source, volume, out, ext, sems = refs
    x = pl.program_id(0)

    @pl.when(x == 0)
    def _():
        planes = [(field.at[:, i], ext.at[:, i + 1, pl.ds(8, CY), :]) for i in range(CX)]
        copies = copies_of(planes, sems)
        start_all(copies)
        edge = jnp.zeros((NVAR, CX + 2, 8, CZ), F32)
        ext[:, :, 0:8, :] = edge
        ext[:, :, 8 + CY : 16 + CY, :] = edge
        plane = jnp.zeros((NVAR, CY, CZ), F32)
        ext[:, 0, 8 : 8 + CY, :] = plane
        ext[:, CX + 1, 8 : 8 + CY, :] = plane
        wait_all(copies)

    lane = lax.broadcasted_iota(jnp.int32, (BAND, CZ), 1)

    def band(i, carry):
        y = pl.multiple_of(i * BAND, BAND)
        flux = [jnp.zeros((BAND, CZ), F32) for _ in range(NVAR)]
        for w in range(NVAR):
            center = ext[w, x + 1, pl.ds(y + 8, BAND), :]
            for d in range(6):
                if d == 0:
                    near = ext[w, x + 2, pl.ds(y + 8, BAND), :]
                elif d == 1:
                    near = ext[w, x, pl.ds(y + 8, BAND), :]
                elif d == 2:
                    near = ext[w, x + 1, pl.ds(y + 9, BAND), :]
                elif d == 3:
                    near = ext[w, x + 1, pl.ds(y + 7, BAND), :]
                elif d == 4:
                    near = jnp.where(lane == CZ - 1, 0.0, pltpu.roll(center, CZ - 1, 1))
                else:
                    near = jnp.where(lane == 0, 0.0, pltpu.roll(center, 1, 1))
                diff = near - center
                for u in range(NVAR):
                    flux[u] = flux[u] + coupling[d, w * NVAR + u] * diff
        vol = volume[0, pl.ds(y, BAND), :]
        for u in range(NVAR):
            rate = vol * flux[u] + source[u, 0, pl.ds(y, BAND), :]
            center = ext[u, x + 1, pl.ds(y + 8, BAND), :]
            if second:
                value = 0.5 * (base[u, 0, pl.ds(y, BAND), :] + center) + (0.5 * TIME_STEP) * rate
            else:
                value = center + TIME_STEP * rate
            out[u, pl.ds(EDGE + x * CY + y, BAND), :] = value
        return carry

    lax.fori_loop(0, CY // BAND, band, 0)

    @pl.when(x == CX - 1)
    def _():
        scale = PENALTY * TIME_STEP * (0.5 if second else 1.0)

        def patch(s, carry):
            t = rows[0, s]
            a, b = t // CY, t % CY
            for v in range(NVAR):
                out[v, pl.ds(t + EDGE, 1), :] -= scale * ext[v, a + 1, pl.ds(b + 8, 1), :]
            return carry

        lax.fori_loop(0, SLOTS, patch, 0)


TABLES = [
    pltpu.SMEM((CAP, PEERS), jnp.int32),
    pltpu.SMEM((1, PEERS), jnp.int32),
    pltpu.SMEM((CAP, PEERS), F32),
]
FIELD_V = pltpu.VMEM((NVAR, ROWS + 2 * EDGE, CZ), F32)
DATA_V = pltpu.VMEM((OTHERS * BLOCKS, PACK, CZ), F32)
ARRIVE = [
    pltpu.SMEM((6, NVAR * NVAR), F32),
    pltpu.SMEM((1, SLOTS), jnp.int32),
    pltpu.VMEM((COMPS, BLOCKS * CAP), jnp.int32),
    DATA_V,
    pltpu.VMEM((NVAR, SLOTS, CZ), F32),
    pltpu.VMEM((NVAR, CY, CZ), F32),
    pltpu.VMEM((NVAR, CY, CZ), F32),
    pltpu.VMEM((2, CY, CZ), F32),
    DMA((7 + OTHERS * LOADS,)),
]


def call(kernel, name, inputs, out_shape, scratch, moved, flops, limit, held=None):
    specs = [HBM] * len(inputs)
    out_specs = [HBM] * len(out_shape)
    aliases = {}
    if held is not None:
        specs[held] = out_specs[0] = VMEM
        aliases = {held: 0}
    return pl.pallas_call(
        kernel,
        in_specs=specs,
        out_specs=out_specs,
        out_shape=out_shape,
        scratch_shapes=scratch,
        input_output_aliases=aliases,
        compiler_params=pltpu.CompilerParams(vmem_limit_bytes=limit),
        cost_estimate=pl.CostEstimate(flops=flops, bytes_accessed=moved, transcendentals=0),
        name=name,
    )(*inputs)


def pack(tables, field):
    (sent,) = call(
        pack_kernel, "pack", [*tables, field], [shape(PEERS, PACK, CZ)],
        [*TABLES, FIELD_V, DATA_V, DMA((3 + NVAR,)), DMA((PIECES,))], 8 << 20, 10**6, WHOLE_VMEM,
    )
    return sent


def middle(tables, field, inputs):
    return call(
        middle_kernel, "middle", [*tables, field, *inputs],
        [FIELD_V, shape(PEERS, PACK, CZ)],
        [*TABLES, *ARRIVE, DMA((3,)), DMA((PIECES,))], 16 << 20, 10**8, VMEM_LIMIT, 3,
    )


def spill(field):
    out_shape = [FIELD_V, shape(NVAR, ROWS, CZ), shape(NVAR, CY, CZ), shape(NVAR, CY, CZ)]
    return call(spill_kernel, "spill", [field], out_shape, [DMA((3,))], 3 << 20, 10**6, VMEM_LIMIT, 0)[1:]


def finish(field, inputs):
    out_shape = [FIELD_V, shape(NVAR, ROWS, CZ)]
    return call(finish_kernel, "finish", [field, *inputs], out_shape, ARRIVE, 10 << 20, 10**8, VMEM_LIMIT, 0)[1]


def advance(second, coupling, rows, field, streams, volume):
    return pl.pallas_call(
        functools.partial(flux_kernel, second),
        grid=(CX,),
        in_specs=[SMEM, SMEM, HBM]
        + [pl.BlockSpec((NVAR, 1, CY, CZ), lambda i: (0, i, 0, 0))] * len(streams)
        + [pl.BlockSpec((1, CY, CZ), lambda i: (i, 0, 0))],
        out_specs=VMEM,
        out_shape=FIELD_V,
        scratch_shapes=[pltpu.VMEM((NVAR, CX + 2, CY + 16, CZ), F32), DMA((CX,))],
        compiler_params=pltpu.CompilerParams(dimension_semantics=("arbitrary",), vmem_limit_bytes=VMEM_LIMIT),
        cost_estimate=pl.CostEstimate(flops=60 * 10**6, bytes_accessed=40 << 20, transcendentals=0),
        name="advance_end" if second else "advance_mid",
    )(coupling, rows, field, *streams, volume)


def exchange(sent):
    return lax.all_to_all(sent, ("comp", "blk"), split_axis=0, concat_axis=0, tiled=True)


def halos(low, high):
    count = lax.axis_size("blk")
    below = lax.ppermute(high, "blk", [(i, i + 1) for i in range(count - 1)])
    above = lax.ppermute(low, "blk", [(i + 1, i) for i in range(count - 1)])
    return below, above


def shards(psi_start, adj_source, vol_inverse, coupling, send_tile, send_count, send_weight, recv_slot, fringe_row):
    start = psi_start[0]
    source = adj_source[0]
    volume = vol_inverse[0]
    matrices = coupling[0].reshape(6, NVAR * NVAR)
    tables = [send_tile[0].T, send_count, send_weight[0].T]
    slots = recv_slot[0].reshape(COMPS, BLOCKS * CAP)

    tiled = (NVAR, ROWS, CZ)

    arrived = exchange(pack(tables, start.reshape(tiled)))
    below, above = halos(start[:, 0], start[:, -1])
    field = advance(False, matrices, fringe_row, start, [source], volume)
    field, sent = middle(tables, field, [matrices, fringe_row, slots, arrived, below, above, volume])
    arrived = exchange(sent)
    mid, low, high = spill(field)
    below, above = halos(low, high)
    field = advance(True, matrices, fringe_row, mid.reshape(NVAR, CX, CY, CZ), [start, source], volume)
    end = finish(field, [matrices, fringe_row, slots, arrived, below, above, volume])
    return end.reshape(1, NVAR, CX, CY, CZ)


def solution(mesh):
    in_specs = (
        P("comp", None, "blk", None, None),
        P("comp", None, "blk", None, None),
        P("comp", "blk", None, None),
        P("comp", None, None, None),
        P(("comp", "blk"), None, None),
        P(("comp", "blk"), None),
        P(("comp", "blk"), None, None),
        P(("comp", "blk"), None, None),
        P(("comp", "blk"), None),
    )
    out_specs = P("comp", None, "blk", None, None)
    return jax.shard_map(shards, mesh=mesh, in_specs=in_specs, out_specs=out_specs, check_vma=False)
```

```python
import functools

import jax
import jax.numpy as jnp
from jax import lax
from jax.experimental import pallas as pl
from jax.experimental.pallas import tpu as pltpu
from jax.sharding import PartitionSpec as P

PENALTY = 4.0
TIME_STEP = 0.08
NVAR, CX, CY, CZ = 6, 8, 128, 128
ROWS = CX * CY
CAP = 8
SLOTS = 64
COMPS = 4
BLOCKS = 32
PEERS = COMPS * BLOCKS
OTHERS = COMPS - 1
PACK = NVAR * CAP
SPLIT = 4
PIECES = OTHERS * SPLIT
BAND = 32
EDGE = 8
BATCH = 8
HALF = 3
WHOLE_VMEM = 67_000_000
VMEM_LIMIT = 63_500_000
F32 = jnp.float32
HBM = pl.BlockSpec(memory_space=pltpu.HBM)
SMEM = pl.BlockSpec(memory_space=pltpu.SMEM)
VMEM = pl.BlockSpec(memory_space=pltpu.VMEM)
DMA = pltpu.SemaphoreType.DMA


def shape(*dims):
    return jax.ShapeDtypeStruct(dims, F32)


def start_all(copies):
    for copy in copies:
        copy.start()


def wait_all(copies):
    for copy in copies:
        copy.wait()


def other(j):
    return lax.rem(lax.axis_index("comp") + j + 1, COMPS)


def block_of(ref, j):
    return ref.at[pl.ds(other(j) * BLOCKS, BLOCKS)]


def part_of(ref, j):
    return ref.at[pl.ds(j * BLOCKS, BLOCKS)]


def gather_rows(field, tables, buf, sent, sems):
    tile, count, weight = tables
    row_ids = lax.broadcasted_iota(jnp.int32, (CAP, CZ), 0)
    size = BLOCKS // SPLIT
    stores = []
    for piece in range(PIECES):
        first = other(piece // SPLIT) * BLOCKS + (piece % SPLIT) * size

        def peer_rows(b, carry):
            peer = first + b
            live = count[0, peer]
            spots = [tile[e, peer] + (EDGE - e) for e in range(CAP)]
            scale = jnp.full((CAP, CZ), weight[0, peer])
            for e in range(1, CAP):
                scale = jnp.where(row_ids == e, weight[e, peer], scale)
            scale = jnp.where(row_ids < live, scale, 0.0)
            for v in range(NVAR):
                rows = field[v, pl.ds(spots[0], CAP), :]
                for e in range(1, CAP):
                    rows = jnp.where(row_ids == e, field[v, pl.ds(spots[e], CAP), :], rows)
                buf[piece * size + b, v * CAP : (v + 1) * CAP, :] = rows * scale
            return carry

        lax.fori_loop(0, size, peer_rows, 0, unroll=8)
        ready = buf.at[pl.ds(piece * size, size)]
        stores.append(pltpu.make_async_copy(ready, sent.at[pl.ds(first, size)], sems.at[piece]))
        stores[-1].start()
    return stores


def reduce_rows(slots, loads, data, total):
    slot_ids = lax.broadcasted_iota(jnp.int32, (SLOTS, BLOCKS * CAP), 0)
    for j in range(OTHERS):
        onehot = (slots[pl.ds(other(j), 1), :] == slot_ids).astype(F32).astype(jnp.bfloat16)
        loads[j].wait()
        for v in range(NVAR):
            part = data[j * BLOCKS : (j + 1) * BLOCKS, v * CAP : (v + 1) * CAP, :].reshape(BLOCKS * CAP, CZ)
            high = part.astype(jnp.bfloat16)
            low = (part - high.astype(F32)).astype(jnp.bfloat16)
            both = jnp.dot(onehot, jnp.concatenate([high, low], axis=1), preferred_element_type=F32)
            both = both[:, :CZ] + both[:, CZ:]
            total[v] = both if j == 0 else total[v] + both


def add_halos(field, coupling, below, above, volume, scale):
    for side, halo, first in ((1, below, EDGE), (0, above, EDGE + ROWS - CY)):

        def band(i, carry):
            y = pl.multiple_of(i * BAND, BAND)
            vol = volume[1 - side, pl.ds(y, BAND), :] * scale
            near = [halo[w, pl.ds(y, BAND), :] for w in range(NVAR)]
            for u in range(NVAR):
                flux = coupling[side, u] * near[0]
                for w in range(1, NVAR):
                    flux = flux + coupling[side, w * NVAR + u] * near[w]
                field[u, pl.ds(first + y, BAND), :] += vol * flux
            return carry

        lax.fori_loop(0, CY // BAND, band, 0)


def patch_rows(field, rows, total, scale, variables):
    def patch(i, carry):
        slots = [i * BATCH + k for k in range(BATCH)]
        spots = [rows[0, s] + EDGE for s in slots]
        sums = []
        for s, t in zip(slots, spots):
            for v in variables:
                sums.append(field[v, pl.ds(t, 1), :] + (PENALTY * scale) * total[v, pl.ds(s, 1), :])
        for k, t in enumerate(spots):
            for n, v in enumerate(variables):
                field[v, pl.ds(t, 1), :] = sums[k * len(variables) + n]
        return carry

    lax.fori_loop(0, SLOTS // BATCH, patch, 0)


def inner(field, first=0, size=ROWS):
    return field.at[:, pl.ds(EDGE + first, size), :]


def line(field, v):
    return field.at[v, pl.ds(EDGE, ROWS), :]


def copies_of(pairs, sems, first=0):
    return [pltpu.make_async_copy(a, b, sems.at[first + i]) for i, (a, b) in enumerate(pairs)]


def pack_kernel(tile, count, weight, field, sent, tile_s, count_s, weight_s, field_v, buf, sems, sent_sems):
    scratch = (tile_s, count_s, weight_s)
    pairs = list(zip((tile, count, weight), scratch)) + [(field.at[v], line(field_v, v)) for v in range(NVAR)]
    copies = copies_of(pairs, sems)
    start_all(copies)
    wait_all(copies)
    wait_all(gather_rows(field_v, scratch, buf, sent, sent_sems))


def arrive(inputs, scratch, sems, field, scale):
    coupling, rows, slots, arrived, below, above, volume = inputs
    coupling_s, rows_s, slots_v, data, total, below_v, above_v, volume_v = scratch
    loads = [(slots, slots_v)] + [(block_of(arrived, j), part_of(data, j)) for j in range(OTHERS)]
    others = [(coupling, coupling_s), (rows, rows_s), (below, below_v), (above, above_v)]
    others += [(volume.at[0], volume_v.at[0]), (volume.at[CX - 1], volume_v.at[1])]
    loads = copies_of(loads, sems)
    others = copies_of(others, sems, len(loads))
    start_all(loads + others)
    loads[0].wait()
    reduce_rows(slots_v, loads[1:], data, total)
    wait_all(others)
    add_halos(field, coupling_s, below_v, above_v, volume_v, scale)


def middle_kernel(*refs):
    tables, inputs, refs = refs[:3], refs[4:11], refs[11:]
    field, sent, low, high, refs = *refs[:4], refs[4:]
    table_scratch, scratch, (sems, table_sems, sent_sems) = refs[:3], refs[3:11], refs[11:]
    table_copies = copies_of(list(zip(tables, table_scratch)), table_sems)
    start_all(table_copies)
    arrive(inputs, scratch, sems, field, TIME_STEP)
    patch_rows(field, scratch[1], scratch[4], TIME_STEP, range(NVAR))
    stores = copies_of([(inner(field, 0, CY), low), (inner(field, ROWS - CY, CY), high)], sems)
    start_all(stores)
    wait_all(table_copies)
    wait_all(gather_rows(field, table_scratch, scratch[3], sent, sent_sems))
    wait_all(stores)


def spill_kernel(field, held, mid, sem):
    store = pltpu.make_async_copy(inner(held), mid, sem)
    store.start()
    store.wait()


def finish_kernel(*refs):
    inputs, (field, end), scratch, sems = refs[1:8], refs[8:10], refs[10:18], refs[18]
    arrive(inputs, scratch, sems, field, 0.5 * TIME_STEP)
    stores = copies_of([(line(field, v), end.at[v]) for v in range(NVAR)], sems)
    for first in range(0, NVAR, HALF):
        half = range(first, first + HALF)
        patch_rows(field, scratch[1], scratch[4], 0.5 * TIME_STEP, half)
        start_all([stores[v] for v in half])
    wait_all(stores)


def flux_kernel(second, coupling, rows, field, *refs):
    if second:
        base, source, volume, out, ext, sems = refs
    else:
        source, volume, out, ext, sems = refs
    x = pl.program_id(0)

    @pl.when(x == 0)
    def _():
        planes = [(field.at[:, i], ext.at[:, i + 1, pl.ds(8, CY), :]) for i in range(CX)]
        copies = copies_of(planes, sems)
        start_all(copies)
        edge = jnp.zeros((NVAR, CX + 2, 8, CZ), F32)
        ext[:, :, 0:8, :] = edge
        ext[:, :, 8 + CY : 16 + CY, :] = edge
        plane = jnp.zeros((NVAR, CY, CZ), F32)
        ext[:, 0, 8 : 8 + CY, :] = plane
        ext[:, CX + 1, 8 : 8 + CY, :] = plane
        wait_all(copies)

    lane = lax.broadcasted_iota(jnp.int32, (BAND, CZ), 1)

    def band(i, carry):
        y = pl.multiple_of(i * BAND, BAND)
        flux = [jnp.zeros((BAND, CZ), F32) for _ in range(NVAR)]
        for w in range(NVAR):
            center = ext[w, x + 1, pl.ds(y + 8, BAND), :]
            for d in range(6):
                if d == 0:
                    near = ext[w, x + 2, pl.ds(y + 8, BAND), :]
                elif d == 1:
                    near = ext[w, x, pl.ds(y + 8, BAND), :]
                elif d == 2:
                    near = ext[w, x + 1, pl.ds(y + 9, BAND), :]
                elif d == 3:
                    near = ext[w, x + 1, pl.ds(y + 7, BAND), :]
                elif d == 4:
                    near = jnp.where(lane == CZ - 1, 0.0, pltpu.roll(center, CZ - 1, 1))
                else:
                    near = jnp.where(lane == 0, 0.0, pltpu.roll(center, 1, 1))
                diff = near - center
                for u in range(NVAR):
                    flux[u] = flux[u] + coupling[d, w * NVAR + u] * diff
        vol = volume[0, pl.ds(y, BAND), :]
        for u in range(NVAR):
            rate = vol * flux[u] + source[u, 0, pl.ds(y, BAND), :]
            center = ext[u, x + 1, pl.ds(y + 8, BAND), :]
            if second:
                value = 0.5 * (base[u, 0, pl.ds(y, BAND), :] + center) + (0.5 * TIME_STEP) * rate
            else:
                value = center + TIME_STEP * rate
            out[u, pl.ds(EDGE + x * CY + y, BAND), :] = value
        return carry

    lax.fori_loop(0, CY // BAND, band, 0)

    @pl.when(x == CX - 1)
    def _():
        scale = PENALTY * TIME_STEP * (0.5 if second else 1.0)

        def patch(s, carry):
            t = rows[0, s]
            a, b = t // CY, t % CY
            for v in range(NVAR):
                out[v, pl.ds(t + EDGE, 1), :] -= scale * ext[v, a + 1, pl.ds(b + 8, 1), :]
            return carry

        lax.fori_loop(0, SLOTS, patch, 0)


TABLES = [
    pltpu.SMEM((CAP, PEERS), jnp.int32),
    pltpu.SMEM((1, PEERS), jnp.int32),
    pltpu.SMEM((CAP, PEERS), F32),
]
FIELD_V = pltpu.VMEM((NVAR, ROWS + 2 * EDGE, CZ), F32)
DATA_V = pltpu.VMEM((OTHERS * BLOCKS, PACK, CZ), F32)
ARRIVE = [
    pltpu.SMEM((6, NVAR * NVAR), F32),
    pltpu.SMEM((1, SLOTS), jnp.int32),
    pltpu.VMEM((COMPS, BLOCKS * CAP), jnp.int32),
    DATA_V,
    pltpu.VMEM((NVAR, SLOTS, CZ), F32),
    pltpu.VMEM((NVAR, CY, CZ), F32),
    pltpu.VMEM((NVAR, CY, CZ), F32),
    pltpu.VMEM((2, CY, CZ), F32),
    DMA((10,)),
]


def call(kernel, name, inputs, out_shape, scratch, moved, flops, limit, held=None):
    specs = [HBM] * len(inputs)
    out_specs = [HBM] * len(out_shape)
    aliases = {}
    if held is not None:
        specs[held] = out_specs[0] = VMEM
        aliases = {held: 0}
    return pl.pallas_call(
        kernel,
        in_specs=specs,
        out_specs=out_specs,
        out_shape=out_shape,
        scratch_shapes=scratch,
        input_output_aliases=aliases,
        compiler_params=pltpu.CompilerParams(vmem_limit_bytes=limit),
        cost_estimate=pl.CostEstimate(flops=flops, bytes_accessed=moved, transcendentals=0),
        name=name,
    )(*inputs)


def pack(tables, field):
    (sent,) = call(
        pack_kernel, "pack", [*tables, field], [shape(PEERS, PACK, CZ)],
        [*TABLES, FIELD_V, DATA_V, DMA((3 + NVAR,)), DMA((PIECES,))], 8 << 20, 10**6, WHOLE_VMEM,
    )
    return sent


def middle(tables, field, inputs):
    return call(
        middle_kernel, "middle", [*tables, field, *inputs],
        [FIELD_V, shape(PEERS, PACK, CZ), shape(NVAR, CY, CZ), shape(NVAR, CY, CZ)],
        [*TABLES, *ARRIVE, DMA((3,)), DMA((PIECES,))], 16 << 20, 10**8, VMEM_LIMIT, 3,
    )


def spill(field):
    out_shape = [FIELD_V, shape(NVAR, ROWS, CZ)]
    return call(spill_kernel, "spill", [field], out_shape, [DMA(())], 3 << 20, 10**6, VMEM_LIMIT, 0)[1]


def finish(field, inputs):
    out_shape = [FIELD_V, shape(NVAR, ROWS, CZ)]
    return call(finish_kernel, "finish", [field, *inputs], out_shape, ARRIVE, 10 << 20, 10**8, VMEM_LIMIT, 0)[1]


def advance(second, coupling, rows, field, streams, volume):
    return pl.pallas_call(
        functools.partial(flux_kernel, second),
        grid=(CX,),
        in_specs=[SMEM, SMEM, HBM]
        + [pl.BlockSpec((NVAR, 1, CY, CZ), lambda i: (0, i, 0, 0))] * len(streams)
        + [pl.BlockSpec((1, CY, CZ), lambda i: (i, 0, 0))],
        out_specs=VMEM,
        out_shape=FIELD_V,
        scratch_shapes=[pltpu.VMEM((NVAR, CX + 2, CY + 16, CZ), F32), DMA((CX,))],
        compiler_params=pltpu.CompilerParams(dimension_semantics=("arbitrary",), vmem_limit_bytes=VMEM_LIMIT),
        cost_estimate=pl.CostEstimate(flops=60 * 10**6, bytes_accessed=40 << 20, transcendentals=0),
        name="advance_end" if second else "advance_mid",
    )(coupling, rows, field, *streams, volume)


def exchange(sent):
    return lax.all_to_all(sent, ("comp", "blk"), split_axis=0, concat_axis=0, tiled=True)


def halos(low, high):
    count = lax.axis_size("blk")
    below = lax.ppermute(high, "blk", [(i, i + 1) for i in range(count - 1)])
    above = lax.ppermute(low, "blk", [(i + 1, i) for i in range(count - 1)])
    return below, above


def shards(psi_start, adj_source, vol_inverse, coupling, send_tile, send_count, send_weight, recv_slot, fringe_row):
    start = psi_start[0]
    source = adj_source[0]
    volume = vol_inverse[0]
    matrices = coupling[0].reshape(6, NVAR * NVAR)
    tables = [send_tile[0].T, send_count, send_weight[0].T]
    slots = recv_slot[0].reshape(COMPS, BLOCKS * CAP)

    tiled = (NVAR, ROWS, CZ)

    arrived = exchange(pack(tables, start.reshape(tiled)))
    below, above = halos(start[:, 0], start[:, -1])
    field = advance(False, matrices, fringe_row, start, [source], volume)
    field, sent, low, high = middle(tables, field, [matrices, fringe_row, slots, arrived, below, above, volume])
    arrived = exchange(sent)
    mid = spill(field)
    below, above = halos(low, high)
    field = advance(True, matrices, fringe_row, mid.reshape(NVAR, CX, CY, CZ), [start, source], volume)
    end = finish(field, [matrices, fringe_row, slots, arrived, below, above, volume])
    return end.reshape(1, NVAR, CX, CY, CZ)


def solution(mesh):
    in_specs = (
        P("comp", None, "blk", None, None),
        P("comp", None, "blk", None, None),
        P("comp", "blk", None, None),
        P("comp", None, None, None),
        P(("comp", "blk"), None, None),
        P(("comp", "blk"), None),
        P(("comp", "blk"), None, None),
        P(("comp", "blk"), None, None),
        P(("comp", "blk"), None),
    )
    out_specs = P("comp", None, "blk", None, None)
    return jax.shard_map(shards, mesh=mesh, in_specs=in_specs, out_specs=out_specs, check_vma=False)
```
